32 devices in a mesh: grp: 8 (over z, x), band: 4 (over y, core).
Axes of the slice: x: 2, y: 2, z: 4, core: 2. Of those that a mesh axis runs over, the one named last changes fastest.
Arguments:
- state: float32 [80, 384, 1280], P('grp', 'band'), may hold values from -6 to 6
- pair_of_slot: int32 [256], replicated, may hold values from 0 to 255, each once
- legendre: float32 [256, 513, 384], P(('grp', 'band')), may hold values from -0.3125 to 0.3125
- diffusion: float32 [80], replicated, may hold values from 0.5 to 8
- w_in: bfloat16 [80, 1024], replicated, may hold values from -0.625 to 0.625
- w_out: bfloat16 [1024, 80], replicated, may hold values from -0.1875 to 0.1875
Outputs:
- new_state: float32 [80, 384, 1280], P('grp', 'band')
The draws below stay inside these ranges and needn't reach their ends.
Inputs may be any that keep to these rules, and one draw needn't show every extreme that they name: `pair_of_slot`: each pair index appears in exactly one slot.
All inputs are finite; a program needn't handle non-finite values.
Results may differ from the reference program's by a relative error of at most 0.004.
Values may be sent and summed in bfloat16 or wider, within the bound.
No kernel may reach another device: no remote copies, remote signals or barrier semaphores. Data moves between devices by JAX's collectives and lax.ppermute only.
A program may use at most 128 MiB of HBM per device.

```python
import math
import jax
import jax.numpy as jnp
from jax import lax

C = 80
NLAT = 384
NLON = 1280
M = 512
HIDDEN_SIZE = 1024
PAIRS = 256


def steps_of(stream_key, dims, cuts, least, largest):
    loudness = 1.0
    for axis_at, blocks in cuts:
        draws = jax.random.uniform(jax.random.fold_in(jax.random.fold_in(stream_key, 6), axis_at), (blocks,), jnp.float32, least / len(cuts), largest / len(cuts))
        loudness = loudness * jnp.repeat(jnp.exp(draws), dims[axis_at] // blocks).reshape((-1,) + (1,) * (len(dims) - 1 - axis_at))
    return loudness


def gaussian(rng, extent, deviation, most, pieces=(), kind=jnp.bfloat16):
    result = jax.random.normal(rng, extent, jnp.float32) * deviation
    if len(pieces) > 0:
        result = steps_of(rng, extent, pieces, -0.22, 0.18) * result
    return jnp.clip(result, min=-most, max=most).astype(kind)


def setup_inputs(seed: int = 0) -> dict:
    key_of = jax.random.split(jax.random.key(seed), 7)
    return {
        "state": gaussian(key_of[0], (C, NLAT, NLON), 1.0, 6.0, ((0, 8), (1, 4)), jnp.float32),
        "pair_of_slot": jax.random.permutation(key_of[1], PAIRS).astype(jnp.int32),
        "legendre": gaussian(key_of[2], (PAIRS, M + 1, NLAT), NLAT ** -0.5, 0.3125, ((0, 32),), jnp.float32),
        "diffusion": jnp.clip(jnp.exp(jax.random.uniform(key_of[3], (C,), jnp.float32, math.log(0.5), math.log(8.0))), 0.5, 8.0),
        "w_in": gaussian(key_of[4], (C, HIDDEN_SIZE), C ** -0.5, 0.625),
        "w_out": gaussian(key_of[5], (HIDDEN_SIZE, C), HIDDEN_SIZE ** -0.5, 0.1875),
    }


def fourier_basis(pair_index, points):
    upper_wave = M - 1 - pair_index
    wavenums = jnp.stack([pair_index, pair_index, upper_wave, upper_wave], axis=1).astype(jnp.int32)
    longitude = jnp.arange(points, dtype=jnp.int32)
    phases = (wavenums[:, :, None] * longitude[None, None, :]) % points
    angles = phases.astype(jnp.float32) * jnp.float32(2.0 * math.pi / points)
    cosine = jnp.cos(angles)
    sine_part = jnp.sin(angles)
    parity = (jnp.arange(4, dtype=jnp.int32) % 2 == 0)[None, :, None]
    forward = jnp.where(parity, cosine, -sine_part) / jnp.float32(points)
    weights = jnp.where(wavenums == 0, jnp.float32(1.0), jnp.float32(2.0))[:, :, None]
    inverse = jnp.where(parity, cosine, -sine_part) * weights
    return forward, inverse


def spectral_step(fields, legendre, pair_index, diffusion):
    projected = jnp.einsum("kjcl,krl->kjcr", fields, legendre, precision=lax.Precision.HIGHEST)
    row_index = jnp.arange(legendre.shape[1], dtype=jnp.int32)
    first_part = row_index[None, :] < (M - pair_index)[:, None]
    degree = jnp.where(first_part, pair_index[:, None] + row_index[None, :], row_index[None, :] - 1).astype(jnp.float32)
    scaled = degree * (degree + 1.0) / jnp.float32(M * (M + 1))
    damping = jnp.exp(-diffusion[None, :, None] * scaled[:, None, :])
    keep_first = first_part[:, None, None, :]
    filtered = jnp.where(keep_first, projected[:, 0:2], projected[:, 2:4]) * damping[:, None]
    nothing = jnp.zeros_like(filtered)
    coeffs = jnp.concatenate([jnp.where(keep_first, filtered, nothing), jnp.where(keep_first, nothing, filtered)], axis=1)
    return jnp.einsum("kjcr,krl->kjcl", coeffs, legendre, precision=lax.Precision.HIGHEST)


def reference(state, pair_of_slot, legendre, diffusion, w_in, w_out):
    forward, inverse = fourier_basis(pair_of_slot, NLON)
    coeffs = jnp.einsum("pjn,cln->pjcl", forward, state, precision=lax.Precision.HIGHEST)

    def per_pair(inputs):
        block, table_rows, pair_index = inputs
        return spectral_step(block[None], table_rows[None], pair_index[None], diffusion)[0]

    grid_coeffs = lax.map(per_pair, (coeffs, legendre, pair_of_slot))
    dynamics = jnp.einsum("pjcl,pjn->cln", grid_coeffs, inverse, precision=lax.Precision.HIGHEST)

    def column_physics(block):
        inputs_low = block.astype(jnp.bfloat16)
        hidden = lax.dot_general(w_in, inputs_low, (((0,), (0,)), ((), ())), preferred_element_type=jnp.float32)
        hidden = jax.nn.silu(hidden).astype(jnp.bfloat16)
        return lax.dot_general(w_out, hidden, (((0,), (0,)), ((), ())), preferred_element_type=jnp.float32)

    tendency = lax.map(column_physics, jnp.moveaxis(state, 1, 0))
    return dynamics + jnp.moveaxis(tendency, 0, 1)
```

```python
import functools
import math

import jax
import jax.numpy as jnp
from jax import lax
from jax.experimental import pallas as pl
from jax.experimental.pallas import tpu as pltpu
from jax.sharding import PartitionSpec as P

LANES = 128
ROWS = 8
F32 = jnp.float32
BF16 = jnp.bfloat16
NT = (((1,), (1,)), ((), ()))
NN = (((1,), (0,)), ((), ()))


def mm(a, b, dims=NN):
    return lax.dot_general(a, b, dims, preferred_element_type=F32)


def halves(value):
    high = value.astype(BF16)
    return high, (value - high.astype(F32)).astype(BF16)


def cost(flops, moved, special=0):
    return pl.CostEstimate(flops=int(flops), bytes_accessed=int(moved), transcendentals=int(special))


def params(mib):
    return pltpu.CompilerParams(dimension_semantics=("arbitrary",), vmem_limit_bytes=mib << 20)


def cut_kernel(tiles, state_ref, out_ref):
    for tile in range(tiles):
        out_ref[0, :, tile] = state_ref[:, :, tile * LANES : (tile + 1) * LANES].astype(BF16)


def cut_columns(state, lat_cuts, lon_cuts):
    chans, lats, lons = state.shape
    rows, tiles = lats // lat_cuts, lons // lon_cuts // LANES
    groups = lat_cuts * lon_cuts
    return pl.pallas_call(
        functools.partial(cut_kernel, tiles),
        grid=(groups,),
        in_specs=[
            pl.BlockSpec((chans, rows, tiles * LANES), lambda g: (0, g // lon_cuts, g % lon_cuts))
        ],
        out_specs=pl.BlockSpec((1, chans, tiles, rows, LANES), lambda g: (g, 0, 0, 0, 0)),
        out_shape=jax.ShapeDtypeStruct((groups, chans, tiles, rows, LANES), BF16),
        compiler_params=params(32),
        cost_estimate=cost(0, state.size * 6),
        name="cut_columns",
    )(state)


def basis_tables(pair_index, points, waves):
    upper = waves - 1 - pair_index
    wavenums = jnp.stack([pair_index, pair_index, upper, upper], axis=1).reshape(-1, 1)
    odd = (jnp.arange(wavenums.shape[0], dtype=jnp.int32) % 2 == 1)[:, None]
    unit = jnp.float32(2.0 * math.pi / points)

    def angles(at):
        return (wavenums * at[None, :] % points).astype(F32) * unit

    fine = angles(jnp.arange(LANES, dtype=jnp.int32))
    coarse = angles(jnp.arange(points // LANES, dtype=jnp.int32) * LANES)
    cosine, sine = jnp.cos(coarse), jnp.sin(coarse)
    by_cos = jnp.where(odd, -sine, cosine)
    by_sin = jnp.where(odd, -cosine, -sine)
    return jnp.cos(fine), jnp.sin(fine), by_cos, by_sin


def forward_kernel(owners, width, folds, state_ref, cos_ref, sin_ref, by_cos_ref, by_sin_ref,
                   out_ref, high_ref, low_ref, state_high, state_low):
    @pl.when(pl.program_id(0) == 0)
    def _():
        state_high[...], state_low[...] = halves(state_ref[...])

    cosine, sine = cos_ref[...], sin_ref[...]
    for tile in range(by_cos_ref.shape[1]):
        at = slice(tile * LANES, (tile + 1) * LANES)
        wave = by_cos_ref[:, tile : tile + 1] * cosine + by_sin_ref[:, tile : tile + 1] * sine
        high_ref[:, at], low_ref[:, at] = halves(wave)
    found = mm(high_ref[...], state_low[...], NT)
    found += mm(low_ref[...], state_high[...], NT)
    found += mm(high_ref[...], state_high[...], NT)
    rows = out_ref.shape[1]
    for owner in range(owners):
        for fold in range(folds):
            start = (owner * folds + fold) * rows
            out_ref[owner, :, fold * width : (fold + 1) * width] = found[start : start + rows].astype(BF16)


def forward_transform(flat, tables, devices, folds, step_rows):
    width, points = flat.shape
    total = tables[0].shape[0]
    per_owner = total // devices
    rows = per_owner // folds
    owners = step_rows // per_owner
    coarse = points // LANES
    return pl.pallas_call(
        functools.partial(forward_kernel, owners, width, folds),
        grid=(total // step_rows,),
        in_specs=[
            pl.BlockSpec((width, points), lambda i: (0, 0)),
            pl.BlockSpec((step_rows, LANES), lambda i: (i, 0)),
            pl.BlockSpec((step_rows, LANES), lambda i: (i, 0)),
            pl.BlockSpec((step_rows, coarse), lambda i: (i, 0)),
            pl.BlockSpec((step_rows, coarse), lambda i: (i, 0)),
        ],
        out_specs=[
            pl.BlockSpec((owners, rows, folds * width), lambda i: (i, 0, 0)),
            pl.BlockSpec((step_rows, points), lambda i: (i, 0)),
            pl.BlockSpec((step_rows, points), lambda i: (i, 0)),
        ],
        out_shape=[
            jax.ShapeDtypeStruct((devices, rows, folds * width), BF16),
            jax.ShapeDtypeStruct((total, points), BF16),
            jax.ShapeDtypeStruct((total, points), BF16),
        ],
        scratch_shapes=[pltpu.VMEM((width, points), BF16), pltpu.VMEM((width, points), BF16)],
        compiler_params=params(56),
        cost_estimate=cost(6 * total * width * points, width * points * 4 + total * (points * 4 + width * 2)),
        name="forward_transform",
    )(flat, *tables)


def physics_kernel(chans, rows, columns_ref, w_in_ref, w_out_ref, out_ref, spread, found):
    spread[...] = columns_ref[...].astype(F32).reshape(chans * rows, LANES)
    for group in range(rows // ROWS):
        at = [pl.ds(group * ROWS + row, chans, stride=rows) for row in range(ROWS)]
        columns = jnp.concatenate([spread[where, :].astype(BF16) for where in at], axis=1)
        half = mm(w_in_ref[...], columns)
        hidden = (half + half * jnp.tanh(half)).astype(BF16)
        tendency = mm(w_out_ref[...], hidden)
        for row in range(ROWS):
            found[at[row], :] = tendency[:, row * LANES : (row + 1) * LANES]
    out_ref[...] = found[...].astype(BF16).reshape(out_ref.shape)


def physics(columns, w_in, w_out):
    groups, per_group, tiles, rows, _ = columns.shape
    chans, hidden = w_in.shape
    spec = pl.BlockSpec((groups, per_group, 1, rows, LANES), lambda i: (0, 0, i, 0, 0))
    count = tiles * rows * LANES
    return pl.pallas_call(
        functools.partial(physics_kernel, chans, rows),
        grid=(tiles,),
        in_specs=[
            spec,
            pl.BlockSpec((hidden, chans), lambda i: (0, 0)),
            pl.BlockSpec((chans, hidden), lambda i: (0, 0)),
        ],
        out_specs=spec,
        out_shape=jax.ShapeDtypeStruct(columns.shape, BF16),
        scratch_shapes=[pltpu.VMEM((chans * rows, LANES), F32), pltpu.VMEM((chans * rows, LANES), F32)],
        compiler_params=params(48),
        cost_estimate=cost(4 * count * chans * hidden, count * chans * 4, count * hidden),
        name="physics",
    )(columns, w_in.T * jnp.asarray(0.5, BF16), w_out.T)


def spectral_kernel(geometry, points, pairs_ref, got_ref, legendre_ref, diffusion_ref, out_ref,
                    rows_ref, block_ref, high_ref, low_ref):
    groups, bands, slots, per_group, lats, folds = geometry
    devices = groups * bands
    per_device = 4 * slots
    fold_rows = per_device // folds
    width = per_group * lats
    degrees = legendre_ref.shape[1]
    waves = degrees - 1
    padded = high_ref.shape[0]
    slot = pl.program_id(0)
    chans = groups * per_group
    spans = [(tile, tile * LANES, min(LANES, width - tile * LANES)) for tile in range(rows_ref.shape[0])]
    fill = rows_ref.shape[0] * LANES - width

    @pl.when(slot == 0)
    def _():
        for device in range(devices):
            for fold in range(folds):
                start = device * per_device + fold * fold_rows
                for tile, at, lanes in spans:
                    rows_ref[tile, start : start + fold_rows, 0:lanes] = got_ref[
                        device, :, fold * width + at : fold * width + at + lanes
                    ].astype(F32)
        high_ref[...] = jnp.zeros_like(high_ref)
        low_ref[...] = jnp.zeros_like(low_ref)

    def rows_of(band, wave):
        return pl.ds(band * per_device + 4 * slot + wave, groups, stride=bands * per_device)

    for wave in range(4):
        for band in range(bands):
            piece = jnp.concatenate([rows_ref[tile, rows_of(band, wave), :] for tile, _, _ in spans], axis=1)
            for chan in range(per_group):
                row = (wave * per_group + chan) * groups
                block_ref[row : row + groups, band * lats : (band + 1) * lats] = piece[
                    :, chan * lats : (chan + 1) * lats
                ]
    high, low = halves(legendre_ref[0])
    high_ref[0:degrees, :] = high
    low_ref[0:degrees, :] = low
    fields = block_ref[...].astype(BF16)
    projected = mm(fields, low_ref[...], NT) + mm(fields, high_ref[...], NT)
    pair = pairs_ref[slot]
    row = lax.broadcasted_iota(jnp.int32, (1, padded), 1)
    first = row < waves - pair
    degree = jnp.where(first, pair + row, row - 1).astype(F32)
    scaled = degree * (degree + 1.0) / F32(waves * (waves + 1))
    wavenum = jnp.where(first, pair, waves - 1 - pair)
    weight = jnp.where(wavenum == 0, F32(1.0 / points), F32(2.0 / points))
    damping = jnp.exp(-diffusion_ref[...] * scaled) * weight
    upper, lower = [], []
    for part in range(2):
        one = projected[part * chans : (part + 1) * chans]
        two = projected[(2 + part) * chans : (3 + part) * chans]
        kept = jnp.where(first, one, two) * damping
        upper.append(jnp.where(first, kept, 0.0))
        lower.append(jnp.where(first, 0.0, kept))
    spec_high, spec_low = halves(jnp.concatenate(upper + lower, axis=0))
    back = mm(spec_low, high_ref[...]) + mm(spec_high, low_ref[...]) + mm(spec_high, high_ref[...])
    for wave in range(4):
        for band in range(bands):
            starts = [(wave * per_group + chan) * groups for chan in range(per_group)]
            pieces = [back[start : start + groups, band * lats : (band + 1) * lats] for start in starts]
            if fill:
                pieces.append(jnp.zeros((groups, fill), F32))
            line = jnp.concatenate(pieces, axis=1)
            for tile, at, _ in spans:
                rows_ref[tile, rows_of(band, wave), :] = line[:, at : at + LANES]

    @pl.when(slot == slots - 1)
    def _():
        for device in range(devices):
            for fold in range(folds):
                start = device * per_device + fold * fold_rows
                for tile, at, lanes in spans:
                    out_ref[device, :, fold * width + at : fold * width + at + lanes] = rows_ref[
                        tile, start : start + fold_rows, 0:lanes
                    ].astype(BF16)


def spectral_step(got, legendre, own_pairs, diffusion, groups, bands, folds, points):
    slots, degrees, lat_total = legendre.shape
    lats = lat_total // bands
    chans = diffusion.shape[0]
    per_group = chans // groups
    padded = -(-degrees // LANES) * LANES
    by_row = diffusion.reshape(groups, per_group).T.reshape(chans, 1)
    geometry = (groups, bands, slots, per_group, lats, folds)
    whole = lambda i, pairs: (0, 0, 0)
    return pl.pallas_call(
        functools.partial(spectral_kernel, geometry, points),
        grid_spec=pltpu.PrefetchScalarGridSpec(
            num_scalar_prefetch=1,
            grid=(slots,),
            in_specs=[
                pl.BlockSpec(got.shape, whole),
                pl.BlockSpec((1, degrees, lat_total), lambda i, pairs: (i, 0, 0)),
                pl.BlockSpec((chans, 1), lambda i, pairs: (0, 0)),
            ],
            out_specs=pl.BlockSpec(got.shape, whole),
            scratch_shapes=[
                pltpu.VMEM((-(-per_group * lats // LANES), groups * bands * 4 * slots, LANES), F32),
                pltpu.VMEM((4 * chans, lat_total), F32),
                pltpu.VMEM((padded, lat_total), BF16),
                pltpu.VMEM((padded, lat_total), BF16),
            ],
        ),
        out_shape=jax.ShapeDtypeStruct(got.shape, BF16),
        compiler_params=params(48),
        cost_estimate=cost(40 * slots * chans * degrees * lat_total, slots * degrees * lat_total * 4),
        name="spectral_step",
    )(own_pairs, got, legendre, by_row)


def inverse_kernel(geometry, back_ref, high_ref, low_ref, tendency_ref, out_ref, rows_ref, turned):
    devices, fold_rows, folds, width, lat_cuts, lon_cuts, tiles = geometry
    chans, lats, step_lons = out_ref.shape
    rows = lats // lat_cuts

    @pl.when(pl.program_id(0) == 0)
    def _():
        rows_ref[...] = jnp.zeros_like(rows_ref)
        for device in range(devices):
            for fold in range(folds):
                start = (device * folds + fold) * fold_rows
                rows_ref[start : start + fold_rows, 0:width] = back_ref[
                    device, :, fold * width : (fold + 1) * width
                ]
        turned[...] = rows_ref[...].T

    waves = turned[0:width, :]
    found = mm(waves, low_ref[...]) + mm(waves, high_ref[...])
    found = found.reshape(chans, lats, step_lons)
    for part in range(step_lons // LANES):
        tile = pl.program_id(0) * (step_lons // LANES) + part
        for cut in range(lat_cuts):
            at = slice(cut * rows, (cut + 1) * rows)
            lanes = slice(part * LANES, (part + 1) * LANES)
            out_ref[:, at, lanes] = found[:, at, lanes] + tendency_ref[
                cut * lon_cuts + tile // tiles, :, tile % tiles
            ].astype(F32)


def inverse_transform(back, high, low, tendency, shape, lat_cuts, lon_cuts, step_lons):
    chans, lats, lons = shape
    devices, fold_rows, wide = back.shape
    width = chans * lats
    folds = wide // width
    total = high.shape[0]
    tiles = tendency.shape[2]
    padded = -(-width // LANES) * LANES
    geometry = (devices, fold_rows, folds, width, lat_cuts, lon_cuts, tiles)
    return pl.pallas_call(
        functools.partial(inverse_kernel, geometry),
        grid=(lons // step_lons,),
        in_specs=[
            pl.BlockSpec(back.shape, lambda i: (0, 0, 0)),
            pl.BlockSpec((total, step_lons), lambda i: (0, i)),
            pl.BlockSpec((total, step_lons), lambda i: (0, i)),
            pl.BlockSpec(tendency.shape, lambda i: (0, 0, 0, 0, 0)),
        ],
        out_specs=pl.BlockSpec((chans, lats, step_lons), lambda i: (0, 0, i)),
        out_shape=jax.ShapeDtypeStruct(shape, F32),
        scratch_shapes=[pltpu.VMEM((total, padded), BF16), pltpu.VMEM((padded, total), BF16)],
        compiler_params=params(56),
        cost_estimate=cost(4 * total * width * lons, total * lons * 4 + width * lons * 6),
        name="inverse_transform",
    )(back, high, low, tendency)


def cuts_of(lats, lons, groups):
    for lon_cuts in range(1, groups + 1):
        if groups % lon_cuts or lons % (lon_cuts * LANES):
            continue
        lat_cuts = groups // lon_cuts
        if lats % (lat_cuts * ROWS) == 0:
            return lat_cuts, lon_cuts
    return None


def folds_of(width, per_device):
    folds = LANES // math.gcd(width, LANES)
    return folds if per_device % (folds * 2 * ROWS) == 0 else None


def fast(state, pair_of_slot, legendre, diffusion, w_in, w_out):
    groups = lax.axis_size("grp")
    bands = lax.axis_size("band")
    devices = groups * bands
    chans, lats, lons = state.shape
    slots, degrees, _ = legendre.shape
    waves = degrees - 1
    lat_cuts, lon_cuts = cuts_of(lats, lons, groups)
    folds = folds_of(chans * lats, 4 * slots)
    cut = cut_columns(state, lat_cuts, lon_cuts)
    cut, pairs = lax.optimization_barrier((cut, pair_of_slot))
    columns = lax.all_to_all(cut, "grp", 0, 0, tiled=True)
    tables = basis_tables(pairs, lons, waves)
    step_rows = min(8, devices) * 4 * slots
    spectra, high, low = forward_transform(state.reshape(chans * lats, lons), tables, devices, folds, step_rows)
    columns, spectra = lax.optimization_barrier((columns, spectra))
    got = lax.all_to_all(spectra, ("grp", "band"), 0, 0, tiled=True)
    tendency = physics(columns, w_in, w_out)
    got, tendency = lax.optimization_barrier((got, tendency))
    tendency = lax.all_to_all(tendency, "grp", 0, 0, tiled=True)
    device = lax.axis_index("grp") * bands + lax.axis_index("band")
    own_pairs = lax.dynamic_slice_in_dim(pairs, device * slots, slots)
    solved = spectral_step(got, legendre, own_pairs, diffusion, groups, bands, folds, lons)
    tendency, solved = lax.optimization_barrier((tendency, solved))
    back = lax.all_to_all(solved, ("grp", "band"), 0, 0, tiled=True)
    return inverse_transform(back, high, low, tendency, state.shape, lat_cuts, lon_cuts, 2 * LANES)


def plain_basis(pair_index, points, waves):
    upper_wave = waves - 1 - pair_index
    wavenums = jnp.stack([pair_index, pair_index, upper_wave, upper_wave], axis=1)
    longitude = jnp.arange(points, dtype=jnp.int32)
    phases = wavenums[:, :, None] * longitude[None, None, :] % points
    angles = phases.astype(jnp.float32) * jnp.float32(2.0 * math.pi / points)
    cosine = jnp.cos(angles)
    sine_part = jnp.sin(angles)
    parity = (jnp.arange(4, dtype=jnp.int32) % 2 == 0)[None, :, None]
    forward = jnp.where(parity, cosine, -sine_part) / jnp.float32(points)
    weights = jnp.where(wavenums == 0, jnp.float32(1.0), jnp.float32(2.0))[:, :, None]
    inverse = jnp.where(parity, cosine, -sine_part) * weights
    return (forward, inverse)


def plain_spectral_step(fields, legendre, pair_index, diffusion):
    waves = legendre.shape[1] - 1
    projected = jnp.einsum("kjcl,krl->kjcr", fields, legendre, precision=lax.Precision.HIGHEST)
    row_index = jnp.arange(legendre.shape[1], dtype=jnp.int32)
    first_part = row_index[None, :] < (waves - pair_index)[:, None]
    degree = jnp.where(
        first_part, pair_index[:, None] + row_index[None, :], row_index[None, :] - 1
    ).astype(jnp.float32)
    scaled = degree * (degree + 1.0) / jnp.float32(waves * (waves + 1))
    damping = jnp.exp(-diffusion[None, :, None] * scaled[:, None, :])
    keep_first = first_part[:, None, None, :]
    filtered = jnp.where(keep_first, projected[:, 0:2], projected[:, 2:4]) * damping[:, None]
    nothing = jnp.zeros_like(filtered)
    coeffs = jnp.concatenate(
        [jnp.where(keep_first, filtered, nothing), jnp.where(keep_first, nothing, filtered)], axis=1
    )
    return jnp.einsum("kjcr,krl->kjcl", coeffs, legendre, precision=lax.Precision.HIGHEST)


def plain(state, pair_of_slot, legendre, diffusion, w_in, w_out):
    groups = lax.axis_size("grp")
    bands = lax.axis_size("band")
    part_chans, lat_rows, lon_total = state.shape
    slot_count = legendre.shape[0]
    lat_total = legendre.shape[2]
    column_block = lax.all_to_all(
        state.astype(jnp.bfloat16), "grp", split_axis=2, concat_axis=0, tiled=True
    )
    channels = column_block.shape[0]
    lon_cols = column_block.shape[2]
    columns = column_block.reshape(channels, lat_rows * lon_cols)
    hidden = lax.dot_general(
        w_in, columns, (((0,), (0,)), ((), ())), preferred_element_type=jnp.float32
    )
    hidden = jax.nn.silu(hidden).astype(jnp.bfloat16)
    tendency = lax.dot_general(
        w_out, hidden, (((0,), (0,)), ((), ())), preferred_element_type=jnp.float32
    )
    tendency = tendency.reshape(channels, lat_rows, lon_cols)
    forward, inverse = plain_basis(pair_of_slot, lon_total, legendre.shape[1] - 1)
    total_slots = forward.shape[0]
    flat_rows = state.reshape(part_chans * lat_rows, lon_total)
    spectra = lax.dot_general(
        forward.reshape(total_slots * 4, lon_total),
        flat_rows,
        (((1,), (1,)), ((), ())),
        precision=lax.Precision.HIGHEST,
    )
    spectra = spectra.reshape(groups, bands, slot_count, 4, part_chans, lat_rows)
    gathered = lax.all_to_all(
        lax.all_to_all(spectra, "grp", split_axis=0, concat_axis=4, tiled=True),
        "band",
        split_axis=1,
        concat_axis=5,
        tiled=True,
    )
    device = lax.axis_index("grp") * bands + lax.axis_index("band")
    own_pairs = lax.dynamic_slice_in_dim(pair_of_slot, device * slot_count, slot_count)
    solved = plain_spectral_step(
        gathered.reshape(slot_count, 4, channels, lat_total), legendre, own_pairs, diffusion
    )
    solved = solved.reshape(1, 1, slot_count, 4, channels, lat_total)
    returned = lax.all_to_all(
        lax.all_to_all(solved, "grp", split_axis=4, concat_axis=0, tiled=True),
        "band",
        split_axis=5,
        concat_axis=1,
        tiled=True,
    )
    coef_flat = returned.reshape(total_slots * 4, part_chans * lat_rows)
    dynamics = lax.dot_general(
        coef_flat,
        inverse.reshape(total_slots * 4, lon_total),
        (((0,), (0,)), ((), ())),
        precision=lax.Precision.HIGHEST,
    )
    dynamics = dynamics.reshape(part_chans, lat_rows, lon_total)
    tendency_rows = lax.all_to_all(
        tendency.astype(jnp.bfloat16), "grp", split_axis=0, concat_axis=2, tiled=True
    ).astype(tendency.dtype)
    return dynamics + tendency_rows


def shards(state, pair_of_slot, legendre, diffusion, w_in, w_out):
    chans, lats, lons = state.shape
    fits = lats % ROWS == 0 and lons % (2 * LANES) == 0
    fits = fits and cuts_of(lats, lons, lax.axis_size("grp")) is not None
    fits = fits and folds_of(chans * lats, 4 * legendre.shape[0]) is not None
    return (fast if fits else plain)(state, pair_of_slot, legendre, diffusion, w_in, w_out)


def solution(mesh):
    return jax.shard_map(
        shards,
        mesh=mesh,
        in_specs=(P("grp", "band", None), P(), P(("grp", "band"), None, None), P(), P(), P()),
        out_specs=P("grp", "band", None),
        check_vma=False,
    )
```

```python
import functools
import math

import jax
import jax.numpy as jnp
from jax import lax
from jax.experimental import pallas as pl
from jax.experimental.pallas import tpu as pltpu
from jax.sharding import PartitionSpec as P


LANES = 128
ROWS = 8
F32 = jnp.float32
BF16 = jnp.bfloat16
NT = (((1,), (1,)), ((), ()))
NN = (((1,), (0,)), ((), ()))


def mm(a, b, dims=NN):
    return lax.dot_general(a, b, dims, preferred_element_type=F32)


def halves(value):
    high = value.astype(BF16)
    return high, (value - high.astype(F32)).astype(BF16)


def cost(flops, moved, special=0):
    return pl.CostEstimate(flops=int(flops), bytes_accessed=int(moved), transcendentals=int(special))


def params(mib):
    return pltpu.CompilerParams(dimension_semantics=("arbitrary",), vmem_limit_bytes=mib << 20)


def cut_kernel(mine_ref, state_ref, *out_refs):
    tiles = out_refs[0].shape[1]
    for offset, out_ref in enumerate(out_refs):

        @pl.when(pl.program_id(0) == offset)
        def _():
            for tile in range(tiles):
                out_ref[:, tile] = state_ref[:, :, tile * LANES : (tile + 1) * LANES].astype(BF16)


def cut_columns(state, mine, lat_cuts, lon_cuts):
    chans, lats, lons = state.shape
    rows, tiles = lats // lat_cuts, lons // lon_cuts // LANES
    groups = lat_cuts * lon_cuts
    block = (chans, tiles, rows, LANES)

    def source(offset, mine):
        group = offset ^ mine[0]
        return (0, group // lon_cuts, group % lon_cuts)

    return pl.pallas_call(
        cut_kernel,
        grid_spec=pltpu.PrefetchScalarGridSpec(
            num_scalar_prefetch=1,
            grid=(groups,),
            in_specs=[pl.BlockSpec((chans, rows, tiles * LANES), source)],
            out_specs=[pl.BlockSpec(block, lambda offset, mine: (0, 0, 0, 0))] * groups,
        ),
        out_shape=[jax.ShapeDtypeStruct(block, BF16)] * groups,
        compiler_params=params(60),
        cost_estimate=cost(0, state.size * 6),
        name="cut_columns",
    )(mine, state)


def exchange(blocks):
    groups = len(blocks)
    got = [blocks[0]] + [None] * (groups - 1)
    for offset in range(groups - 1, 0, -1):
        got[offset] = lax.ppermute(blocks[offset], "grp", [(g, g ^ offset) for g in range(groups)])
    return got


def basis_tables(pair_index, points, waves):
    upper = waves - 1 - pair_index
    wavenums = jnp.stack([pair_index, pair_index, upper, upper], axis=1).reshape(-1, 1)
    odd = (jnp.arange(wavenums.shape[0], dtype=jnp.int32) % 2 == 1)[:, None]
    unit = jnp.float32(2.0 * math.pi / points)

    def angles(at):
        return (wavenums * at[None, :] % points).astype(F32) * unit

    fine = angles(jnp.arange(LANES, dtype=jnp.int32))
    coarse = angles(jnp.arange(points // LANES, dtype=jnp.int32) * LANES)
    cosine, sine = jnp.cos(coarse), jnp.sin(coarse)
    by_cos = jnp.where(odd, -sine, cosine)
    by_sin = jnp.where(odd, -cosine, -sine)
    return jnp.cos(fine), jnp.sin(fine), by_cos, by_sin


def forward_kernel(owners, width, folds, state_ref, cos_ref, sin_ref, by_cos_ref, by_sin_ref,
                   out_ref, high_ref, low_ref, state_high, state_low):
    @pl.when(pl.program_id(0) == 0)
    def _():
        state_high[...], state_low[...] = halves(state_ref[...])

    cosine, sine = cos_ref[...], sin_ref[...]
    for tile in range(by_cos_ref.shape[1]):
        at = slice(tile * LANES, (tile + 1) * LANES)
        wave = by_cos_ref[:, tile : tile + 1] * cosine + by_sin_ref[:, tile : tile + 1] * sine
        high_ref[:, at], low_ref[:, at] = halves(wave)
    found = mm(high_ref[...], state_low[...], NT)
    found += mm(low_ref[...], state_high[...], NT)
    found += mm(high_ref[...], state_high[...], NT)
    rows = out_ref.shape[1]
    for owner in range(owners):
        for fold in range(folds):
            start = (owner * folds + fold) * rows
            out_ref[owner, :, fold * width : (fold + 1) * width] = found[start : start + rows].astype(BF16)


def forward_transform(flat, tables, devices, folds, step_rows):
    width, points = flat.shape
    total = tables[0].shape[0]
    per_owner = total // devices
    rows = per_owner // folds
    owners = step_rows // per_owner
    coarse = points // LANES
    return pl.pallas_call(
        functools.partial(forward_kernel, owners, width, folds),
        grid=(total // step_rows,),
        in_specs=[
            pl.BlockSpec((width, points), lambda i: (0, 0)),
            pl.BlockSpec((step_rows, LANES), lambda i: (i, 0)),
            pl.BlockSpec((step_rows, LANES), lambda i: (i, 0)),
            pl.BlockSpec((step_rows, coarse), lambda i: (i, 0)),
            pl.BlockSpec((step_rows, coarse), lambda i: (i, 0)),
        ],
        out_specs=[
            pl.BlockSpec((owners, rows, folds * width), lambda i: (i, 0, 0)),
            pl.BlockSpec((step_rows, points), lambda i: (i, 0)),
            pl.BlockSpec((step_rows, points), lambda i: (i, 0)),
        ],
        out_shape=[
            jax.ShapeDtypeStruct((devices, rows, folds * width), BF16),
            jax.ShapeDtypeStruct((total, points), BF16),
            jax.ShapeDtypeStruct((total, points), BF16),
        ],
        scratch_shapes=[pltpu.VMEM((width, points), BF16), pltpu.VMEM((width, points), BF16)],
        compiler_params=params(56),
        cost_estimate=cost(6 * total * width * points, width * points * 4 + total * (points * 4 + width * 2)),
        name="forward_transform",
    )(flat, *tables)


def physics_kernel(groups, mine_ref, *refs):
    columns, (w_in_ref, w_out_ref) = refs[:groups], refs[groups : groups + 2]
    outs, (spread, found) = refs[groups + 2 : 2 * groups + 2], refs[2 * groups + 2 :]
    per_group, _, rows, _ = columns[0].shape
    chans = groups * per_group
    span = per_group * rows

    def part(offset):
        return pl.ds(pl.multiple_of((mine_ref[0] ^ offset) * span, ROWS), span)

    for offset in range(groups):
        spread[part(offset), :] = columns[offset][:, 0].astype(F32).reshape(span, LANES)
    for group in range(rows // ROWS):
        at = [pl.ds(group * ROWS + row, chans, stride=rows) for row in range(ROWS)]
        block = jnp.concatenate([spread[where, :].astype(BF16) for where in at], axis=1)
        half = mm(w_in_ref[...], block)
        hidden = (half + half * jnp.tanh(half)).astype(BF16)
        tendency = mm(w_out_ref[...], hidden)
        for row in range(ROWS):
            found[at[row], :] = tendency[:, row * LANES : (row + 1) * LANES]
    for offset in range(groups):
        outs[offset][:, 0] = found[part(offset), :].astype(BF16).reshape(per_group, rows, LANES)


def physics(columns, mine, w_in, w_out):
    groups = len(columns)
    per_group, tiles, rows, _ = columns[0].shape
    chans, hidden = w_in.shape
    spec = pl.BlockSpec((per_group, 1, rows, LANES), lambda i, mine: (0, i, 0, 0))
    count = tiles * rows * LANES
    return pl.pallas_call(
        functools.partial(physics_kernel, groups),
        grid_spec=pltpu.PrefetchScalarGridSpec(
            num_scalar_prefetch=1,
            grid=(tiles,),
            in_specs=[spec] * groups
            + [
                pl.BlockSpec((hidden, chans), lambda i, mine: (0, 0)),
                pl.BlockSpec((chans, hidden), lambda i, mine: (0, 0)),
            ],
            out_specs=[spec] * groups,
            scratch_shapes=[pltpu.VMEM((chans * rows, LANES), F32), pltpu.VMEM((chans * rows, LANES), F32)],
        ),
        out_shape=[jax.ShapeDtypeStruct(columns[0].shape, BF16)] * groups,
        compiler_params=params(48),
        cost_estimate=cost(4 * count * chans * hidden, count * chans * 4, count * hidden),
        name="physics",
    )(mine, *columns, w_in.T * jnp.asarray(0.5, BF16), w_out.T)


def gather_kernel(mine_ref, *refs):
    for offset, part in enumerate(refs[:-1]):
        refs[-1][mine_ref[0] ^ offset] = part[...]


def gather_tendency(parts, mine):
    groups = len(parts)
    shape = parts[0].shape
    return pl.pallas_call(
        gather_kernel,
        grid_spec=pltpu.PrefetchScalarGridSpec(
            num_scalar_prefetch=1,
            grid=(1,),
            in_specs=[pl.BlockSpec(shape, lambda i, mine: (0, 0, 0, 0))] * groups,
            out_specs=pl.BlockSpec((groups,) + shape, lambda i, mine: (0, 0, 0, 0, 0)),
        ),
        out_shape=jax.ShapeDtypeStruct((groups,) + shape, BF16),
        compiler_params=params(48),
        cost_estimate=cost(0, 4 * groups * parts[0].size),
        name="gather_tendency",
    )(mine, *parts)


def spectral_kernel(geometry, points, pairs_ref, got_ref, legendre_ref, diffusion_ref, out_ref,
                    rows_ref, block_ref, high_ref, low_ref):
    groups, bands, slots, per_group, lats, folds = geometry
    devices = groups * bands
    per_device = 4 * slots
    fold_rows = per_device // folds
    width = per_group * lats
    degrees = legendre_ref.shape[1]
    waves = degrees - 1
    padded = high_ref.shape[0]
    slot = pl.program_id(0)
    chans = groups * per_group
    spans = [(tile, tile * LANES, min(LANES, width - tile * LANES)) for tile in range(rows_ref.shape[0])]
    fill = rows_ref.shape[0] * LANES - width

    @pl.when(slot == 0)
    def _():
        for device in range(devices):
            for fold in range(folds):
                start = device * per_device + fold * fold_rows
                for tile, at, lanes in spans:
                    rows_ref[tile, start : start + fold_rows, 0:lanes] = got_ref[
                        device, :, fold * width + at : fold * width + at + lanes
                    ].astype(F32)
        high_ref[...] = jnp.zeros_like(high_ref)
        low_ref[...] = jnp.zeros_like(low_ref)

    def rows_of(band, wave):
        return pl.ds(band * per_device + 4 * slot + wave, groups, stride=bands * per_device)

    for wave in range(4):
        for band in range(bands):
            piece = jnp.concatenate([rows_ref[tile, rows_of(band, wave), :] for tile, _, _ in spans], axis=1)
            for chan in range(per_group):
                row = (wave * per_group + chan) * groups
                block_ref[row : row + groups, band * lats : (band + 1) * lats] = piece[
                    :, chan * lats : (chan + 1) * lats
                ]
    high, low = halves(legendre_ref[0])
    high_ref[0:degrees, :] = high
    low_ref[0:degrees, :] = low
    fields = block_ref[...].astype(BF16)
    projected = mm(fields, low_ref[...], NT) + mm(fields, high_ref[...], NT)
    pair = pairs_ref[slot]
    row = lax.broadcasted_iota(jnp.int32, (1, padded), 1)
    first = row < waves - pair
    degree = jnp.where(first, pair + row, row - 1).astype(F32)
    scaled = degree * (degree + 1.0) / F32(waves * (waves + 1))
    wavenum = jnp.where(first, pair, waves - 1 - pair)
    weight = jnp.where(wavenum == 0, F32(1.0 / points), F32(2.0 / points))
    damping = jnp.exp(-diffusion_ref[...] * scaled) * weight
    upper, lower = [], []
    for part in range(2):
        one = projected[part * chans : (part + 1) * chans]
        two = projected[(2 + part) * chans : (3 + part) * chans]
        kept = jnp.where(first, one, two) * damping
        upper.append(jnp.where(first, kept, 0.0))
        lower.append(jnp.where(first, 0.0, kept))
    spec_high, spec_low = halves(jnp.concatenate(upper + lower, axis=0))
    back = mm(spec_low, high_ref[...]) + mm(spec_high, low_ref[...]) + mm(spec_high, high_ref[...])
    for wave in range(4):
        for band in range(bands):
            starts = [(wave * per_group + chan) * groups for chan in range(per_group)]
            pieces = [back[start : start + groups, band * lats : (band + 1) * lats] for start in starts]
            if fill:
                pieces.append(jnp.zeros((groups, fill), F32))
            line = jnp.concatenate(pieces, axis=1)
            for tile, at, _ in spans:
                rows_ref[tile, rows_of(band, wave), :] = line[:, at : at + LANES]

    @pl.when(slot == slots - 1)
    def _():
        for device in range(devices):
            for fold in range(folds):
                start = device * per_device + fold * fold_rows
                for tile, at, lanes in spans:
                    out_ref[device, :, fold * width + at : fold * width + at + lanes] = rows_ref[
                        tile, start : start + fold_rows, 0:lanes
                    ].astype(BF16)


def spectral_step(got, legendre, own_pairs, diffusion, groups, bands, folds, points):
    slots, degrees, lat_total = legendre.shape
    lats = lat_total // bands
    chans = diffusion.shape[0]
    per_group = chans // groups
    padded = -(-degrees // LANES) * LANES
    by_row = diffusion.reshape(groups, per_group).T.reshape(chans, 1)
    geometry = (groups, bands, slots, per_group, lats, folds)
    whole = lambda i, pairs: (0, 0, 0)
    return pl.pallas_call(
        functools.partial(spectral_kernel, geometry, points),
        grid_spec=pltpu.PrefetchScalarGridSpec(
            num_scalar_prefetch=1,
            grid=(slots,),
            in_specs=[
                pl.BlockSpec(got.shape, whole),
                pl.BlockSpec((1, degrees, lat_total), lambda i, pairs: (i, 0, 0)),
                pl.BlockSpec((chans, 1), lambda i, pairs: (0, 0)),
            ],
            out_specs=pl.BlockSpec(got.shape, whole),
            scratch_shapes=[
                pltpu.VMEM((-(-per_group * lats // LANES), groups * bands * 4 * slots, LANES), F32),
                pltpu.VMEM((4 * chans, lat_total), F32),
                pltpu.VMEM((padded, lat_total), BF16),
                pltpu.VMEM((padded, lat_total), BF16),
            ],
        ),
        out_shape=jax.ShapeDtypeStruct(got.shape, BF16),
        compiler_params=params(48),
        cost_estimate=cost(40 * slots * chans * degrees * lat_total, slots * degrees * lat_total * 4),
        name="spectral_step",
    )(own_pairs, got, legendre, by_row)


def inverse_kernel(geometry, back_ref, high_ref, low_ref, tendency_ref, out_ref, rows_ref, turned):
    devices, fold_rows, folds, width, lat_cuts, lon_cuts, tiles = geometry
    chans, lats, step_lons = out_ref.shape
    rows = lats // lat_cuts

    @pl.when(pl.program_id(0) == 0)
    def _():
        rows_ref[...] = jnp.zeros_like(rows_ref)
        for device in range(devices):
            for fold in range(folds):
                start = (device * folds + fold) * fold_rows
                rows_ref[start : start + fold_rows, 0:width] = back_ref[
                    device, :, fold * width : (fold + 1) * width
                ]
        turned[...] = rows_ref[...].T

    waves = turned[0:width, :]
    found = mm(waves, low_ref[...]) + mm(waves, high_ref[...])
    found = found.reshape(chans, lats, step_lons)
    for part in range(step_lons // LANES):
        tile = pl.program_id(0) * (step_lons // LANES) + part
        for cut in range(lat_cuts):
            at = slice(cut * rows, (cut + 1) * rows)
            lanes = slice(part * LANES, (part + 1) * LANES)
            out_ref[:, at, lanes] = found[:, at, lanes] + tendency_ref[
                cut * lon_cuts + tile // tiles, :, tile % tiles
            ].astype(F32)


def inverse_transform(back, high, low, tendency, shape, lat_cuts, lon_cuts, step_lons):
    chans, lats, lons = shape
    devices, fold_rows, wide = back.shape
    width = chans * lats
    folds = wide // width
    total = high.shape[0]
    tiles = tendency.shape[2]
    padded = -(-width // LANES) * LANES
    geometry = (devices, fold_rows, folds, width, lat_cuts, lon_cuts, tiles)
    return pl.pallas_call(
        functools.partial(inverse_kernel, geometry),
        grid=(lons // step_lons,),
        in_specs=[
            pl.BlockSpec(back.shape, lambda i: (0, 0, 0)),
            pl.BlockSpec((total, step_lons), lambda i: (0, i)),
            pl.BlockSpec((total, step_lons), lambda i: (0, i)),
            pl.BlockSpec(tendency.shape, lambda i: (0, 0, 0, 0, 0)),
        ],
        out_specs=pl.BlockSpec((chans, lats, step_lons), lambda i: (0, 0, i)),
        out_shape=jax.ShapeDtypeStruct(shape, F32),
        scratch_shapes=[pltpu.VMEM((total, padded), BF16), pltpu.VMEM((padded, total), BF16)],
        compiler_params=params(56),
        cost_estimate=cost(4 * total * width * lons, total * lons * 4 + width * lons * 6),
        name="inverse_transform",
    )(back, high, low, tendency)


def cuts_of(lats, lons, groups):
    for lon_cuts in range(1, groups + 1):
        if groups % lon_cuts or lons % (lon_cuts * LANES):
            continue
        lat_cuts = groups // lon_cuts
        if lats % (lat_cuts * ROWS) == 0:
            return lat_cuts, lon_cuts
    return None


def folds_of(width, per_device):
    folds = LANES // math.gcd(width, LANES)
    return folds if per_device % (folds * 2 * ROWS) == 0 else None


def fast(state, pair_of_slot, legendre, diffusion, w_in, w_out):
    groups = lax.axis_size("grp")
    bands = lax.axis_size("band")
    devices = groups * bands
    chans, lats, lons = state.shape
    slots, degrees, _ = legendre.shape
    waves = degrees - 1
    lat_cuts, lon_cuts = cuts_of(lats, lons, groups)
    folds = folds_of(chans * lats, 4 * slots)
    mine = lax.axis_index("grp")
    device = mine * bands + lax.axis_index("band")
    mine = mine.reshape(1)
    cut = cut_columns(state, mine, lat_cuts, lon_cuts)
    *cut, pairs = lax.optimization_barrier((*cut, pair_of_slot))
    columns = exchange(cut)
    tables = basis_tables(pairs, lons, waves)
    step_rows = min(8, devices) * 4 * slots
    spectra, high, low = forward_transform(state.reshape(chans * lats, lons), tables, devices, folds, step_rows)
    got = lax.all_to_all(spectra, ("grp", "band"), 0, 0, tiled=True)
    tendency = physics(columns, mine, w_in, w_out)
    *tendency, pairs = lax.optimization_barrier((*tendency, pairs))
    tendency = exchange(tendency)
    own_pairs = lax.dynamic_slice_in_dim(pairs, device * slots, slots)
    solved = spectral_step(got, legendre, own_pairs, diffusion, groups, bands, folds, lons)
    back = lax.all_to_all(solved, ("grp", "band"), 0, 0, tiled=True)
    tendency = gather_tendency(tendency, mine)
    return inverse_transform(back, high, low, tendency, state.shape, lat_cuts, lon_cuts, 2 * LANES)


def plain_basis(pair_index, points, waves):
    upper_wave = waves - 1 - pair_index
    wavenums = jnp.stack([pair_index, pair_index, upper_wave, upper_wave], axis=1)
    longitude = jnp.arange(points, dtype=jnp.int32)
    phases = wavenums[:, :, None] * longitude[None, None, :] % points
    angles = phases.astype(jnp.float32) * jnp.float32(2.0 * math.pi / points)
    cosine = jnp.cos(angles)
    sine_part = jnp.sin(angles)
    parity = (jnp.arange(4, dtype=jnp.int32) % 2 == 0)[None, :, None]
    forward = jnp.where(parity, cosine, -sine_part) / jnp.float32(points)
    weights = jnp.where(wavenums == 0, jnp.float32(1.0), jnp.float32(2.0))[:, :, None]
    inverse = jnp.where(parity, cosine, -sine_part) * weights
    return (forward, inverse)


def plain_spectral_step(fields, legendre, pair_index, diffusion):
    waves = legendre.shape[1] - 1
    projected = jnp.einsum("kjcl,krl->kjcr", fields, legendre, precision=lax.Precision.HIGHEST)
    row_index = jnp.arange(legendre.shape[1], dtype=jnp.int32)
    first_part = row_index[None, :] < (waves - pair_index)[:, None]
    degree = jnp.where(
        first_part, pair_index[:, None] + row_index[None, :], row_index[None, :] - 1
    ).astype(jnp.float32)
    scaled = degree * (degree + 1.0) / jnp.float32(waves * (waves + 1))
    damping = jnp.exp(-diffusion[None, :, None] * scaled[:, None, :])
    keep_first = first_part[:, None, None, :]
    filtered = jnp.where(keep_first, projected[:, 0:2], projected[:, 2:4]) * damping[:, None]
    nothing = jnp.zeros_like(filtered)
    coeffs = jnp.concatenate(
        [jnp.where(keep_first, filtered, nothing), jnp.where(keep_first, nothing, filtered)], axis=1
    )
    return jnp.einsum("kjcr,krl->kjcl", coeffs, legendre, precision=lax.Precision.HIGHEST)


def plain(state, pair_of_slot, legendre, diffusion, w_in, w_out):
    groups = lax.axis_size("grp")
    bands = lax.axis_size("band")
    part_chans, lat_rows, lon_total = state.shape
    slot_count = legendre.shape[0]
    lat_total = legendre.shape[2]
    column_block = lax.all_to_all(
        state.astype(jnp.bfloat16), "grp", split_axis=2, concat_axis=0, tiled=True
    )
    channels = column_block.shape[0]
    lon_cols = column_block.shape[2]
    columns = column_block.reshape(channels, lat_rows * lon_cols)
    hidden = lax.dot_general(
        w_in, columns, (((0,), (0,)), ((), ())), preferred_element_type=jnp.float32
    )
    hidden = jax.nn.silu(hidden).astype(jnp.bfloat16)
    tendency = lax.dot_general(
        w_out, hidden, (((0,), (0,)), ((), ())), preferred_element_type=jnp.float32
    )
    tendency = tendency.reshape(channels, lat_rows, lon_cols)
    forward, inverse = plain_basis(pair_of_slot, lon_total, legendre.shape[1] - 1)
    total_slots = forward.shape[0]
    flat_rows = state.reshape(part_chans * lat_rows, lon_total)
    spectra = lax.dot_general(
        forward.reshape(total_slots * 4, lon_total),
        flat_rows,
        (((1,), (1,)), ((), ())),
        precision=lax.Precision.HIGHEST,
    )
    spectra = spectra.reshape(groups, bands, slot_count, 4, part_chans, lat_rows)
    gathered = lax.all_to_all(
        lax.all_to_all(spectra, "grp", split_axis=0, concat_axis=4, tiled=True),
        "band",
        split_axis=1,
        concat_axis=5,
        tiled=True,
    )
    device = lax.axis_index("grp") * bands + lax.axis_index("band")
    own_pairs = lax.dynamic_slice_in_dim(pair_of_slot, device * slot_count, slot_count)
    solved = plain_spectral_step(
        gathered.reshape(slot_count, 4, channels, lat_total), legendre, own_pairs, diffusion
    )
    solved = solved.reshape(1, 1, slot_count, 4, channels, lat_total)
    returned = lax.all_to_all(
        lax.all_to_all(solved, "grp", split_axis=4, concat_axis=0, tiled=True),
        "band",
        split_axis=5,
        concat_axis=1,
        tiled=True,
    )
    coef_flat = returned.reshape(total_slots * 4, part_chans * lat_rows)
    dynamics = lax.dot_general(
        coef_flat,
        inverse.reshape(total_slots * 4, lon_total),
        (((0,), (0,)), ((), ())),
        precision=lax.Precision.HIGHEST,
    )
    dynamics = dynamics.reshape(part_chans, lat_rows, lon_total)
    tendency_rows = lax.all_to_all(
        tendency.astype(jnp.bfloat16), "grp", split_axis=0, concat_axis=2, tiled=True
    ).astype(tendency.dtype)
    return dynamics + tendency_rows


def shards(state, pair_of_slot, legendre, diffusion, w_in, w_out):
    chans, lats, lons = state.shape
    groups = lax.axis_size("grp")
    fits = groups & (groups - 1) == 0 and lats % ROWS == 0 and lons % (2 * LANES) == 0
    fits = fits and cuts_of(lats, lons, groups) is not None
    fits = fits and folds_of(chans * lats, 4 * legendre.shape[0]) is not None
    if not fits:
        return plain(state, pair_of_slot, legendre, diffusion, w_in, w_out)
    return fast(state, pair_of_slot, legendre, diffusion, w_in, w_out)


def solution(mesh):
    return jax.shard_map(
        shards,
        mesh=mesh,
        in_specs=(P("grp", "band", None), P(), P(("grp", "band"), None, None), P(), P(), P()),
        out_specs=P("grp", "band", None),
        check_vma=False,
    )
```

```python
import functools
import math

import jax
import jax.numpy as jnp
from jax import lax
from jax.experimental import pallas as pl
from jax.experimental.pallas import tpu as pltpu
from jax.sharding import PartitionSpec as P


LANES = 128
ROWS = 8
F32 = jnp.float32
BF16 = jnp.bfloat16
NT = (((1,), (1,)), ((), ()))
NN = (((1,), (0,)), ((), ()))


def mm(a, b, dims=NN):
    return lax.dot_general(a, b, dims, preferred_element_type=F32)


def halves(value):
    high = value.astype(BF16)
    return high, (value - high.astype(F32)).astype(BF16)


def cost(flops, moved, special=0):
    return pl.CostEstimate(flops=int(flops), bytes_accessed=int(moved), transcendentals=int(special))


def params(mib):
    return pltpu.CompilerParams(dimension_semantics=("arbitrary",), vmem_limit_bytes=mib << 20)


def cut_kernel(lon_cuts, mine_ref, state_ref, *refs):
    groups = len(refs) - 4
    out_refs, (wide, narrow, arrived, left) = refs[:groups], refs[groups:]
    _, tiles, rows, _ = out_refs[0].shape
    lons = tiles * LANES

    def fetch(offset):
        group = mine_ref[0] ^ offset
        lat = pl.multiple_of(group // lon_cuts * rows, ROWS)
        lon = pl.multiple_of(group % lon_cuts * lons, LANES)
        block = state_ref.at[:, pl.ds(lat, rows), pl.ds(lon, lons)]
        return pltpu.make_async_copy(block, wide.at[offset], arrived.at[offset])

    def store(offset):
        return pltpu.make_async_copy(narrow.at[offset], out_refs[offset], left.at[offset])

    for offset in range(groups):
        fetch(offset).start()
    for offset in range(groups):
        fetch(offset).wait()
        for tile in range(tiles):
            narrow[offset, :, tile] = wide[offset, :, :, tile * LANES : (tile + 1) * LANES].astype(BF16)
        store(offset).start()
    for offset in range(groups):
        store(offset).wait()


def cut_columns(state, mine, lat_cuts, lon_cuts):
    chans, lats, lons = state.shape
    rows, tiles = lats // lat_cuts, lons // lon_cuts // LANES
    groups = lat_cuts * lon_cuts
    block = (chans, tiles, rows, LANES)
    return pl.pallas_call(
        functools.partial(cut_kernel, lon_cuts),
        grid_spec=pltpu.PrefetchScalarGridSpec(
            num_scalar_prefetch=1,
            grid=(1,),
            in_specs=[pl.BlockSpec(memory_space=pl.ANY)],
            out_specs=[pl.BlockSpec(memory_space=pl.ANY)] * groups,
            scratch_shapes=[
                pltpu.VMEM((groups, chans, rows, tiles * LANES), F32),
                pltpu.VMEM((groups,) + block, BF16),
                pltpu.SemaphoreType.DMA((groups,)),
                pltpu.SemaphoreType.DMA((groups,)),
            ],
        ),
        out_shape=[jax.ShapeDtypeStruct(block, BF16)] * groups,
        compiler_params=params(60),
        cost_estimate=cost(0, state.size * 6),
        name="cut_columns",
    )(mine, state)


def exchange(blocks):
    groups = len(blocks)
    got = [blocks[0]] + [None] * (groups - 1)
    for offset in range(groups - 1, 0, -1):
        got[offset] = lax.ppermute(blocks[offset], "grp", [(g, g ^ offset) for g in range(groups)])
    return got


def basis_tables(pair_index, points, waves):
    upper = waves - 1 - pair_index
    wavenums = jnp.stack([pair_index, pair_index, upper, upper], axis=1).reshape(-1, 1)
    odd = (jnp.arange(wavenums.shape[0], dtype=jnp.int32) % 2 == 1)[:, None]
    unit = jnp.float32(2.0 * math.pi / points)

    def angles(at):
        return (wavenums * at[None, :] % points).astype(F32) * unit

    fine = angles(jnp.arange(LANES, dtype=jnp.int32))
    coarse = angles(jnp.arange(points // LANES, dtype=jnp.int32) * LANES)
    cosine, sine = jnp.cos(coarse), jnp.sin(coarse)
    by_cos = jnp.where(odd, -sine, cosine)
    by_sin = jnp.where(odd, -cosine, -sine)
    return jnp.cos(fine), jnp.sin(fine), by_cos, by_sin


def forward_kernel(owners, width, folds, state_ref, cos_ref, sin_ref, by_cos_ref, by_sin_ref,
                   out_ref, high_ref, low_ref, state_high, state_low):
    @pl.when(pl.program_id(0) == 0)
    def _():
        state_high[...], state_low[...] = halves(state_ref[...])

    cosine, sine = cos_ref[...], sin_ref[...]
    for tile in range(by_cos_ref.shape[1]):
        at = slice(tile * LANES, (tile + 1) * LANES)
        wave = by_cos_ref[:, tile : tile + 1] * cosine + by_sin_ref[:, tile : tile + 1] * sine
        high_ref[:, at], low_ref[:, at] = halves(wave)
    found = mm(high_ref[...], state_low[...], NT)
    found += mm(low_ref[...], state_high[...], NT)
    found += mm(high_ref[...], state_high[...], NT)
    rows = out_ref.shape[1]
    for owner in range(owners):
        for fold in range(folds):
            start = (owner * folds + fold) * rows
            out_ref[owner, :, fold * width : (fold + 1) * width] = found[start : start + rows].astype(BF16)


def forward_transform(flat, tables, devices, folds, step_rows):
    width, points = flat.shape
    total = tables[0].shape[0]
    per_owner = total // devices
    rows = per_owner // folds
    owners = step_rows // per_owner
    coarse = points // LANES
    return pl.pallas_call(
        functools.partial(forward_kernel, owners, width, folds),
        grid=(total // step_rows,),
        in_specs=[
            pl.BlockSpec((width, points), lambda i: (0, 0)),
            pl.BlockSpec((step_rows, LANES), lambda i: (i, 0)),
            pl.BlockSpec((step_rows, LANES), lambda i: (i, 0)),
            pl.BlockSpec((step_rows, coarse), lambda i: (i, 0)),
            pl.BlockSpec((step_rows, coarse), lambda i: (i, 0)),
        ],
        out_specs=[
            pl.BlockSpec((owners, rows, folds * width), lambda i: (i, 0, 0)),
            pl.BlockSpec((step_rows, points), lambda i: (i, 0)),
        ],
        out_shape=[
            jax.ShapeDtypeStruct((devices, rows, folds * width), BF16),
            jax.ShapeDtypeStruct((total, points), BF16),
        ],
        scratch_shapes=[
            pltpu.VMEM((step_rows, points), BF16),
            pltpu.VMEM((width, points), BF16),
            pltpu.VMEM((width, points), BF16),
        ],
        compiler_params=params(56),
        cost_estimate=cost(6 * total * width * points, width * points * 4 + total * (points * 4 + width * 2)),
        name="forward_transform",
    )(flat, *tables)


def physics_kernel(groups, mine_ref, *refs):
    columns, (w_in_ref, w_out_ref) = refs[:groups], refs[groups : groups + 2]
    outs, (spread, found) = refs[groups + 2 : 2 * groups + 2], refs[2 * groups + 2 :]
    per_group, _, rows, _ = columns[0].shape
    chans = groups * per_group
    span = per_group * rows

    def part(offset):
        return pl.ds(pl.multiple_of((mine_ref[0] ^ offset) * span, ROWS), span)

    for offset in range(groups):
        spread[part(offset), :] = columns[offset][:, 0].astype(F32).reshape(span, LANES)
    for group in range(rows // ROWS):
        at = [pl.ds(group * ROWS + row, chans, stride=rows) for row in range(ROWS)]
        block = jnp.concatenate([spread[where, :].astype(BF16) for where in at], axis=1)
        half = mm(w_in_ref[...], block)
        hidden = (half + half * jnp.tanh(half)).astype(BF16)
        tendency = mm(w_out_ref[...], hidden)
        for row in range(ROWS):
            found[at[row], :] = tendency[:, row * LANES : (row + 1) * LANES]
    for offset in range(groups):
        outs[offset][:, 0] = found[part(offset), :].astype(BF16).reshape(per_group, rows, LANES)


def physics(columns, mine, w_in, w_out):
    groups = len(columns)
    per_group, tiles, rows, _ = columns[0].shape
    chans, hidden = w_in.shape
    spec = pl.BlockSpec((per_group, 1, rows, LANES), lambda i, mine: (0, i, 0, 0))
    count = tiles * rows * LANES
    return pl.pallas_call(
        functools.partial(physics_kernel, groups),
        grid_spec=pltpu.PrefetchScalarGridSpec(
            num_scalar_prefetch=1,
            grid=(tiles,),
            in_specs=[spec] * groups
            + [
                pl.BlockSpec((hidden, chans), lambda i, mine: (0, 0)),
                pl.BlockSpec((chans, hidden), lambda i, mine: (0, 0)),
            ],
            out_specs=[spec] * groups,
            scratch_shapes=[pltpu.VMEM((chans * rows, LANES), F32), pltpu.VMEM((chans * rows, LANES), F32)],
        ),
        out_shape=[jax.ShapeDtypeStruct(columns[0].shape, BF16)] * groups,
        compiler_params=params(48),
        cost_estimate=cost(4 * count * chans * hidden, count * chans * 4, count * hidden),
        name="physics",
    )(mine, *columns, w_in.T * jnp.asarray(0.5, BF16), w_out.T)


def gather_kernel(lon_cuts, mine_ref, *refs):
    out_ref = refs[-1]
    tiles = refs[0].shape[1]
    for offset, part in enumerate(refs[:-1]):
        group = mine_ref[0] ^ offset
        for tile in range(tiles):
            out_ref[group % lon_cuts * tiles + tile, group // lon_cuts] = part[:, tile]


def gather_tendency(parts, mine, lat_cuts, lon_cuts):
    shape = parts[0].shape
    chans, tiles, rows, _ = shape
    out = (lon_cuts * tiles, lat_cuts, chans, rows, LANES)
    return pl.pallas_call(
        functools.partial(gather_kernel, lon_cuts),
        grid_spec=pltpu.PrefetchScalarGridSpec(
            num_scalar_prefetch=1,
            grid=(1,),
            in_specs=[pl.BlockSpec(shape, lambda i, mine: (0, 0, 0, 0))] * len(parts),
            out_specs=pl.BlockSpec(out, lambda i, mine: (0, 0, 0, 0, 0)),
        ),
        out_shape=jax.ShapeDtypeStruct(out, BF16),
        compiler_params=params(48),
        cost_estimate=cost(0, 4 * len(parts) * parts[0].size),
        name="gather_tendency",
    )(mine, *parts)


def spectral_kernel(geometry, points, pairs_ref, got_ref, legendre_ref, diffusion_ref, out_ref,
                    rows_ref, block_ref, high_ref, low_ref):
    groups, bands, slots, per_group, lats, folds = geometry
    devices = groups * bands
    per_device = 4 * slots
    fold_rows = per_device // folds
    width = per_group * lats
    degrees = legendre_ref.shape[1]
    waves = degrees - 1
    padded = high_ref.shape[0]
    slot = pl.program_id(0)
    chans = groups * per_group
    spans = [(tile, tile * LANES, min(LANES, width - tile * LANES)) for tile in range(rows_ref.shape[0])]
    fill = rows_ref.shape[0] * LANES - width

    @pl.when(slot == 0)
    def _():
        for device in range(devices):
            for fold in range(folds):
                start = device * per_device + fold * fold_rows
                for tile, at, lanes in spans:
                    rows_ref[tile, start : start + fold_rows, 0:lanes] = got_ref[
                        device, :, fold * width + at : fold * width + at + lanes
                    ].astype(F32)
        high_ref[...] = jnp.zeros_like(high_ref)
        low_ref[...] = jnp.zeros_like(low_ref)

    def rows_of(band, wave):
        return pl.ds(band * per_device + 4 * slot + wave, groups, stride=bands * per_device)

    for wave in range(4):
        for band in range(bands):
            piece = jnp.concatenate([rows_ref[tile, rows_of(band, wave), :] for tile, _, _ in spans], axis=1)
            for chan in range(per_group):
                row = (wave * per_group + chan) * groups
                block_ref[row : row + groups, band * lats : (band + 1) * lats] = piece[
                    :, chan * lats : (chan + 1) * lats
                ]
    high, low = halves(legendre_ref[0])
    high_ref[0:degrees, :] = high
    low_ref[0:degrees, :] = low
    fields = block_ref[...].astype(BF16)
    projected = mm(fields, low_ref[...], NT) + mm(fields, high_ref[...], NT)
    pair = pairs_ref[slot]
    row = lax.broadcasted_iota(jnp.int32, (1, padded), 1)
    first = row < waves - pair
    degree = jnp.where(first, pair + row, row - 1).astype(F32)
    scaled = degree * (degree + 1.0) / F32(waves * (waves + 1))
    wavenum = jnp.where(first, pair, waves - 1 - pair)
    weight = jnp.where(wavenum == 0, F32(1.0 / points), F32(2.0 / points))
    damping = jnp.exp(-diffusion_ref[...] * scaled) * weight
    upper, lower = [], []
    for part in range(2):
        one = projected[part * chans : (part + 1) * chans]
        two = projected[(2 + part) * chans : (3 + part) * chans]
        kept = jnp.where(first, one, two) * damping
        upper.append(jnp.where(first, kept, 0.0))
        lower.append(jnp.where(first, 0.0, kept))
    spec_high, spec_low = halves(jnp.concatenate(upper + lower, axis=0))
    back = mm(spec_low, high_ref[...]) + mm(spec_high, low_ref[...]) + mm(spec_high, high_ref[...])
    for wave in range(4):
        for band in range(bands):
            starts = [(wave * per_group + chan) * groups for chan in range(per_group)]
            pieces = [back[start : start + groups, band * lats : (band + 1) * lats] for start in starts]
            if fill:
                pieces.append(jnp.zeros((groups, fill), F32))
            line = jnp.concatenate(pieces, axis=1)
            for tile, at, _ in spans:
                rows_ref[tile, rows_of(band, wave), :] = line[:, at : at + LANES]

    @pl.when(slot == slots - 1)
    def _():
        for device in range(devices):
            for fold in range(folds):
                start = device * per_device + fold * fold_rows
                for tile, at, lanes in spans:
                    out_ref[device, :, fold * width + at : fold * width + at + lanes] = rows_ref[
                        tile, start : start + fold_rows, 0:lanes
                    ].astype(BF16)


def spectral_step(got, legendre, own_pairs, diffusion, groups, bands, folds, points):
    slots, degrees, lat_total = legendre.shape
    lats = lat_total // bands
    chans = diffusion.shape[0]
    per_group = chans // groups
    padded = -(-degrees // LANES) * LANES
    by_row = diffusion.reshape(groups, per_group).T.reshape(chans, 1)
    geometry = (groups, bands, slots, per_group, lats, folds)
    whole = lambda i, pairs: (0, 0, 0)
    return pl.pallas_call(
        functools.partial(spectral_kernel, geometry, points),
        grid_spec=pltpu.PrefetchScalarGridSpec(
            num_scalar_prefetch=1,
            grid=(slots,),
            in_specs=[
                pl.BlockSpec(got.shape, whole),
                pl.BlockSpec((1, degrees, lat_total), lambda i, pairs: (i, 0, 0)),
                pl.BlockSpec((chans, 1), lambda i, pairs: (0, 0)),
            ],
            out_specs=pl.BlockSpec(got.shape, whole),
            scratch_shapes=[
                pltpu.VMEM((-(-per_group * lats // LANES), groups * bands * 4 * slots, LANES), F32),
                pltpu.VMEM((4 * chans, lat_total), F32),
                pltpu.VMEM((padded, lat_total), BF16),
                pltpu.VMEM((padded, lat_total), BF16),
            ],
        ),
        out_shape=jax.ShapeDtypeStruct(got.shape, BF16),
        compiler_params=params(48),
        cost_estimate=cost(40 * slots * chans * degrees * lat_total, slots * degrees * lat_total * 4),
        name="spectral_step",
    )(own_pairs, got, legendre, by_row)


def inverse_kernel(geometry, back_ref, basis_ref, tendency_ref, out_ref, rows_ref, turned):
    devices, fold_rows, folds, width = geometry
    chans, lats, step_lons = out_ref.shape
    _, lat_cuts, _, rows, _ = tendency_ref.shape

    @pl.when(pl.program_id(0) == 0)
    def _():
        rows_ref[...] = jnp.zeros_like(rows_ref)
        for device in range(devices):
            for fold in range(folds):
                start = (device * folds + fold) * fold_rows
                rows_ref[start : start + fold_rows, 0:width] = back_ref[
                    device, :, fold * width : (fold + 1) * width
                ]
        turned[...] = rows_ref[...].T

    waves = turned[0:width, :]
    found = mm(waves, basis_ref[...])
    found = found.reshape(chans, lats, step_lons)
    for part in range(step_lons // LANES):
        for cut in range(lat_cuts):
            at = slice(cut * rows, (cut + 1) * rows)
            lanes = slice(part * LANES, (part + 1) * LANES)
            out_ref[:, at, lanes] = found[:, at, lanes] + tendency_ref[part, cut].astype(F32)


def inverse_transform(back, basis, tendency, shape, step_lons):
    chans, lats, lons = shape
    devices, fold_rows, wide = back.shape
    width = chans * lats
    folds = wide // width
    total = basis.shape[0]
    padded = -(-width // LANES) * LANES
    geometry = (devices, fold_rows, folds, width)
    return pl.pallas_call(
        functools.partial(inverse_kernel, geometry),
        grid=(lons // step_lons,),
        in_specs=[
            pl.BlockSpec(back.shape, lambda i: (0, 0, 0), pipeline_mode=pl.Buffered(1)),
            pl.BlockSpec((total, step_lons), lambda i: (0, i)),
            pl.BlockSpec((step_lons // LANES,) + tendency.shape[1:], lambda i: (i, 0, 0, 0, 0)),
        ],
        out_specs=pl.BlockSpec((chans, lats, step_lons), lambda i: (0, 0, i)),
        out_shape=jax.ShapeDtypeStruct(shape, F32),
        scratch_shapes=[pltpu.VMEM((total, padded), BF16), pltpu.VMEM((padded, total), BF16)],
        compiler_params=params(48),
        cost_estimate=cost(2 * total * width * lons, total * lons * 2 + width * lons * 6),
        name="inverse_transform",
    )(back, basis, tendency)


def cuts_of(lats, lons, groups):
    for lon_cuts in range(1, groups + 1):
        if groups % lon_cuts or lons % (lon_cuts * LANES):
            continue
        lat_cuts = groups // lon_cuts
        if lats % (lat_cuts * ROWS) == 0:
            return lat_cuts, lon_cuts
    return None


def folds_of(width, per_device):
    folds = LANES // math.gcd(width, LANES)
    return folds if per_device % (folds * 2 * ROWS) == 0 else None


def fast(state, pair_of_slot, legendre, diffusion, w_in, w_out):
    groups = lax.axis_size("grp")
    bands = lax.axis_size("band")
    devices = groups * bands
    chans, lats, lons = state.shape
    slots, degrees, _ = legendre.shape
    waves = degrees - 1
    lat_cuts, lon_cuts = cuts_of(lats, lons, groups)
    folds = folds_of(chans * lats, 4 * slots)
    mine = lax.axis_index("grp")
    device = mine * bands + lax.axis_index("band")
    mine = mine.reshape(1)
    cut = cut_columns(state, mine, lat_cuts, lon_cuts)
    *cut, pairs = lax.optimization_barrier((*cut, pair_of_slot))
    columns = exchange(cut)
    tables = basis_tables(pairs, lons, waves)
    step_rows = min(8, devices) * 4 * slots
    spectra, basis = forward_transform(state.reshape(chans * lats, lons), tables, devices, folds, step_rows)
    got = lax.all_to_all(spectra, ("grp", "band"), 0, 0, tiled=True)
    tendency = physics(columns, mine, w_in, w_out)
    *tendency, pairs = lax.optimization_barrier((*tendency, pairs))
    tendency = exchange(tendency)
    own_pairs = lax.dynamic_slice_in_dim(pairs, device * slots, slots)
    solved = spectral_step(got, legendre, own_pairs, diffusion, groups, bands, folds, lons)
    back = lax.all_to_all(solved, ("grp", "band"), 0, 0, tiled=True)
    tendency = gather_tendency(tendency, mine, lat_cuts, lon_cuts)
    return inverse_transform(back, basis, tendency, state.shape, 2 * LANES)


def plain_basis(pair_index, points, waves):
    upper_wave = waves - 1 - pair_index
    wavenums = jnp.stack([pair_index, pair_index, upper_wave, upper_wave], axis=1)
    longitude = jnp.arange(points, dtype=jnp.int32)
    phases = wavenums[:, :, None] * longitude[None, None, :] % points
    angles = phases.astype(jnp.float32) * jnp.float32(2.0 * math.pi / points)
    cosine = jnp.cos(angles)
    sine_part = jnp.sin(angles)
    parity = (jnp.arange(4, dtype=jnp.int32) % 2 == 0)[None, :, None]
    forward = jnp.where(parity, cosine, -sine_part) / jnp.float32(points)
    weights = jnp.where(wavenums == 0, jnp.float32(1.0), jnp.float32(2.0))[:, :, None]
    inverse = jnp.where(parity, cosine, -sine_part) * weights
    return (forward, inverse)


def plain_spectral_step(fields, legendre, pair_index, diffusion):
    waves = legendre.shape[1] - 1
    projected = jnp.einsum("kjcl,krl->kjcr", fields, legendre, precision=lax.Precision.HIGHEST)
    row_index = jnp.arange(legendre.shape[1], dtype=jnp.int32)
    first_part = row_index[None, :] < (waves - pair_index)[:, None]
    degree = jnp.where(
        first_part, pair_index[:, None] + row_index[None, :], row_index[None, :] - 1
    ).astype(jnp.float32)
    scaled = degree * (degree + 1.0) / jnp.float32(waves * (waves + 1))
    damping = jnp.exp(-diffusion[None, :, None] * scaled[:, None, :])
    keep_first = first_part[:, None, None, :]
    filtered = jnp.where(keep_first, projected[:, 0:2], projected[:, 2:4]) * damping[:, None]
    nothing = jnp.zeros_like(filtered)
    coeffs = jnp.concatenate(
        [jnp.where(keep_first, filtered, nothing), jnp.where(keep_first, nothing, filtered)], axis=1
    )
    return jnp.einsum("kjcr,krl->kjcl", coeffs, legendre, precision=lax.Precision.HIGHEST)


def plain(state, pair_of_slot, legendre, diffusion, w_in, w_out):
    groups = lax.axis_size("grp")
    bands = lax.axis_size("band")
    part_chans, lat_rows, lon_total = state.shape
    slot_count = legendre.shape[0]
    lat_total = legendre.shape[2]
    column_block = lax.all_to_all(
        state.astype(jnp.bfloat16), "grp", split_axis=2, concat_axis=0, tiled=True
    )
    channels = column_block.shape[0]
    lon_cols = column_block.shape[2]
    columns = column_block.reshape(channels, lat_rows * lon_cols)
    hidden = lax.dot_general(
        w_in, columns, (((0,), (0,)), ((), ())), preferred_element_type=jnp.float32
    )
    hidden = jax.nn.silu(hidden).astype(jnp.bfloat16)
    tendency = lax.dot_general(
        w_out, hidden, (((0,), (0,)), ((), ())), preferred_element_type=jnp.float32
    )
    tendency = tendency.reshape(channels, lat_rows, lon_cols)
    forward, inverse = plain_basis(pair_of_slot, lon_total, legendre.shape[1] - 1)
    total_slots = forward.shape[0]
    flat_rows = state.reshape(part_chans * lat_rows, lon_total)
    spectra = lax.dot_general(
        forward.reshape(total_slots * 4, lon_total),
        flat_rows,
        (((1,), (1,)), ((), ())),
        precision=lax.Precision.HIGHEST,
    )
    spectra = spectra.reshape(groups, bands, slot_count, 4, part_chans, lat_rows)
    gathered = lax.all_to_all(
        lax.all_to_all(spectra, "grp", split_axis=0, concat_axis=4, tiled=True),
        "band",
        split_axis=1,
        concat_axis=5,
        tiled=True,
    )
    device = lax.axis_index("grp") * bands + lax.axis_index("band")
    own_pairs = lax.dynamic_slice_in_dim(pair_of_slot, device * slot_count, slot_count)
    solved = plain_spectral_step(
        gathered.reshape(slot_count, 4, channels, lat_total), legendre, own_pairs, diffusion
    )
    solved = solved.reshape(1, 1, slot_count, 4, channels, lat_total)
    returned = lax.all_to_all(
        lax.all_to_all(solved, "grp", split_axis=4, concat_axis=0, tiled=True),
        "band",
        split_axis=5,
        concat_axis=1,
        tiled=True,
    )
    coef_flat = returned.reshape(total_slots * 4, part_chans * lat_rows)
    dynamics = lax.dot_general(
        coef_flat,
        inverse.reshape(total_slots * 4, lon_total),
        (((0,), (0,)), ((), ())),
        precision=lax.Precision.HIGHEST,
    )
    dynamics = dynamics.reshape(part_chans, lat_rows, lon_total)
    tendency_rows = lax.all_to_all(
        tendency.astype(jnp.bfloat16), "grp", split_axis=0, concat_axis=2, tiled=True
    ).astype(tendency.dtype)
    return dynamics + tendency_rows


def shards(state, pair_of_slot, legendre, diffusion, w_in, w_out):
    chans, lats, lons = state.shape
    groups = lax.axis_size("grp")
    fits = groups & (groups - 1) == 0 and lats % ROWS == 0 and lons % (2 * LANES) == 0
    fits = fits and cuts_of(lats, lons, groups) is not None
    fits = fits and folds_of(chans * lats, 4 * legendre.shape[0]) is not None
    if not fits:
        return plain(state, pair_of_slot, legendre, diffusion, w_in, w_out)
    return fast(state, pair_of_slot, legendre, diffusion, w_in, w_out)


def solution(mesh):
    return jax.shard_map(
        shards,
        mesh=mesh,
        in_specs=(P("grp", "band", None), P(), P(("grp", "band"), None, None), P(), P(), P()),
        out_specs=P("grp", "band", None),
        check_vma=False,
    )
```

```python
import functools
import math

import jax
import jax.numpy as jnp
from jax import lax
from jax.experimental import pallas as pl
from jax.experimental.pallas import tpu as pltpu
from jax.sharding import PartitionSpec as P


LANES = 128
ROWS = 8
F32 = jnp.float32
BF16 = jnp.bfloat16
NT = (((1,), (1,)), ((), ()))
NN = (((1,), (0,)), ((), ()))


def mm(a, b, dims=NN):
    return lax.dot_general(a, b, dims, preferred_element_type=F32)


def halves(value):
    high = value.astype(BF16)
    return high, (value - high.astype(F32)).astype(BF16)


def cost(flops, moved, special=0):
    return pl.CostEstimate(flops=int(flops), bytes_accessed=int(moved), transcendentals=int(special))


def params(mib):
    return pltpu.CompilerParams(dimension_semantics=("arbitrary",), vmem_limit_bytes=mib << 20)


def cut_kernel(lon_cuts, mine_ref, state_ref, *refs):
    groups = len(refs) - 4
    out_refs, (wide, narrow, arrived, left) = refs[:groups], refs[groups:]
    _, tiles, rows, _ = out_refs[0].shape
    lons = tiles * LANES

    def fetch(offset):
        group = mine_ref[0] ^ offset
        lat = pl.multiple_of(group // lon_cuts * rows, ROWS)
        lon = pl.multiple_of(group % lon_cuts * lons, LANES)
        block = state_ref.at[:, pl.ds(lat, rows), pl.ds(lon, lons)]
        return pltpu.make_async_copy(block, wide.at[offset], arrived.at[offset])

    def store(offset):
        return pltpu.make_async_copy(narrow.at[offset], out_refs[offset], left.at[offset])

    for offset in range(groups):
        fetch(offset).start()
    for offset in range(groups):
        fetch(offset).wait()
        for tile in range(tiles):
            narrow[offset, :, tile] = wide[offset, :, :, tile * LANES : (tile + 1) * LANES].astype(BF16)
        store(offset).start()
    for offset in range(groups):
        store(offset).wait()


def cut_columns(state, mine, lat_cuts, lon_cuts):
    chans, lats, lons = state.shape
    rows, tiles = lats // lat_cuts, lons // lon_cuts // LANES
    groups = lat_cuts * lon_cuts
    block = (chans, tiles, rows, LANES)
    return pl.pallas_call(
        functools.partial(cut_kernel, lon_cuts),
        grid_spec=pltpu.PrefetchScalarGridSpec(
            num_scalar_prefetch=1,
            grid=(1,),
            in_specs=[pl.BlockSpec(memory_space=pl.ANY)],
            out_specs=[pl.BlockSpec(memory_space=pl.ANY)] * groups,
            scratch_shapes=[
                pltpu.VMEM((groups, chans, rows, tiles * LANES), F32),
                pltpu.VMEM((groups,) + block, BF16),
                pltpu.SemaphoreType.DMA((groups,)),
                pltpu.SemaphoreType.DMA((groups,)),
            ],
        ),
        out_shape=[jax.ShapeDtypeStruct(block, BF16)] * groups,
        compiler_params=params(60),
        cost_estimate=cost(0, state.size * 6),
        name="cut_columns",
    )(mine, state)


def exchange(blocks):
    groups = len(blocks)
    got = [blocks[0]] + [None] * (groups - 1)
    for offset in range(groups - 1, 0, -1):
        got[offset] = lax.ppermute(blocks[offset], "grp", [(g, g ^ offset) for g in range(groups)])
    return got


def basis_tables(pair_index, points, waves):
    upper = waves - 1 - pair_index
    wavenums = jnp.stack([pair_index, pair_index, upper, upper], axis=1).reshape(-1, 1)
    odd = (jnp.arange(wavenums.shape[0], dtype=jnp.int32) % 2 == 1)[:, None]
    unit = jnp.float32(2.0 * math.pi / points)

    def angles(at):
        return (wavenums * at[None, :] % points).astype(F32) * unit

    fine = angles(jnp.arange(LANES, dtype=jnp.int32))
    coarse = angles(jnp.arange(points // LANES, dtype=jnp.int32) * LANES)
    cosine, sine = jnp.cos(coarse), jnp.sin(coarse)
    by_cos = jnp.where(odd, -sine, cosine)
    by_sin = jnp.where(odd, -cosine, -sine)
    return jnp.cos(fine), jnp.sin(fine), by_cos, by_sin


def forward_kernel(owners, folds, half_ref, state_ref, cos_ref, sin_ref, by_cos_ref, by_sin_ref,
                   near_ref, far_ref, high_ref, low_ref, state_high, state_low):
    chans, lats, points = state_ref.shape
    part = lats // 2
    width = chans * part
    half = half_ref[0]

    @pl.when(pl.program_id(0) == 0)
    def _():
        for side in range(2):
            at = slice(side * width, (side + 1) * width)
            rows = pl.ds(pl.multiple_of((half ^ side) * part, ROWS), part)
            block = state_ref[:, rows, :].reshape(width, points)
            state_high[at, :], state_low[at, :] = halves(block)

    cosine, sine = cos_ref[...], sin_ref[...]
    for tile in range(by_cos_ref.shape[1]):
        at = slice(tile * LANES, (tile + 1) * LANES)
        wave = by_cos_ref[:, tile : tile + 1] * cosine + by_sin_ref[:, tile : tile + 1] * sine
        high_ref[:, at], low_ref[:, at] = halves(wave)
    found = mm(high_ref[...], state_low[...], NT)
    found += mm(low_ref[...], state_high[...], NT)
    found += mm(high_ref[...], state_high[...], NT)
    rows = near_ref.shape[1]

    def put(out_ref, lane):
        for owner in range(owners):
            for fold in range(folds):
                start = (owner * folds + fold) * rows
                out_ref[owner, :, fold * width : (fold + 1) * width] = found[
                    start : start + rows, lane : lane + width
                ].astype(BF16)

    put(near_ref, 0)

    @pl.when(pl.program_id(0) // (pl.num_programs(0) // 2) == half)
    def _():
        put(far_ref, width)


def forward_transform(state, half, tables, devices, folds, step_rows):
    chans, lats, points = state.shape
    width = chans * lats
    total = tables[0].shape[0]
    per_owner = total // devices
    rows = per_owner // folds
    owners = step_rows // per_owner
    steps = total // step_rows
    coarse = points // LANES
    wide = folds * width // 2

    def own_half(i, half):
        return (jnp.clip(i - half[0] * (steps // 2), 0, steps // 2 - 1), 0, 0)

    return pl.pallas_call(
        functools.partial(forward_kernel, owners, folds),
        grid_spec=pltpu.PrefetchScalarGridSpec(
            num_scalar_prefetch=1,
            grid=(steps,),
            in_specs=[
                pl.BlockSpec((chans, lats, points), lambda i, half: (0, 0, 0)),
                pl.BlockSpec((step_rows, LANES), lambda i, half: (i, 0)),
                pl.BlockSpec((step_rows, LANES), lambda i, half: (i, 0)),
                pl.BlockSpec((step_rows, coarse), lambda i, half: (i, 0)),
                pl.BlockSpec((step_rows, coarse), lambda i, half: (i, 0)),
            ],
            out_specs=[
                pl.BlockSpec((owners, rows, wide), lambda i, half: (i, 0, 0)),
                pl.BlockSpec((owners, rows, wide), own_half),
                pl.BlockSpec((step_rows, points), lambda i, half: (i, 0)),
            ],
            scratch_shapes=[
                pltpu.VMEM((step_rows, points), BF16),
                pltpu.VMEM((width, points), BF16),
                pltpu.VMEM((width, points), BF16),
            ],
        ),
        out_shape=[
            jax.ShapeDtypeStruct((devices, rows, wide), BF16),
            jax.ShapeDtypeStruct((devices // 2, rows, wide), BF16),
            jax.ShapeDtypeStruct((total, points), BF16),
        ],
        compiler_params=params(56),
        cost_estimate=cost(6 * total * width * points, width * points * 4 + total * (points * 4 + width * 2)),
        name="forward_transform",
    )(half, state, *tables)


def cross_kernel(owners, mine_ref, *refs):
    blocks, (basis_ref, far_ref, out_ref, columns) = refs[:-4], refs[-4:]
    quads = len(blocks)
    chans, tiles, rows, _ = blocks[0].shape
    span = chans * rows
    far_rows = far_ref.shape[1]
    cross_rows = out_ref.shape[1] - far_rows
    folds = out_ref.shape[2] // span
    per_owner = basis_ref.shape[0] // owners

    @pl.when(pl.program_id(0) == 0)
    def _():
        for offset, block in enumerate(blocks):
            place = pl.ds(pl.multiple_of((mine_ref[0] % quads ^ offset) * span, 2 * ROWS), span)
            for tile in range(tiles):
                columns[place, tile * LANES : (tile + 1) * LANES] = block[:, tile].reshape(span, LANES)

    found = mm(basis_ref[...], columns[...], NT)
    per_quad = per_owner // cross_rows
    for owner in range(owners):
        out_ref[owner, cross_rows : cross_rows + far_rows, :] = far_ref[owner]
        for fold in range(folds):
            quad, start = fold // per_quad, owner * per_owner + fold % per_quad * cross_rows
            out_ref[owner, 0:cross_rows, fold * span : (fold + 1) * span] = found[
                start : start + cross_rows, quad * span : (quad + 1) * span
            ].astype(BF16)


def cross_transform(blocks, far, basis, mine, devices, lon_cuts, step_rows):
    quads = len(blocks)
    chans, tiles, rows, _ = blocks[0].shape
    span = chans * rows
    per_owner = basis.shape[0] // devices
    owners = step_rows // per_owner
    steps = devices // 2 // owners
    cross_rows = quads * per_owner * span // far.shape[2]
    out = (devices // 2, cross_rows + far.shape[1], far.shape[2])
    return pl.pallas_call(
        functools.partial(cross_kernel, owners),
        grid_spec=pltpu.PrefetchScalarGridSpec(
            num_scalar_prefetch=1,
            grid=(steps,),
            in_specs=[pl.BlockSpec(blocks[0].shape, lambda i, mine: (0, 0, 0, 0))] * quads
            + [
                pl.BlockSpec(
                    (step_rows, tiles * LANES), lambda i, mine: (mine[0] // quads * steps + i, mine[0] % lon_cuts)
                ),
                pl.BlockSpec((owners,) + far.shape[1:], lambda i, mine: (i, 0, 0)),
            ],
            out_specs=pl.BlockSpec((owners,) + out[1:], lambda i, mine: (i, 0, 0)),
            scratch_shapes=[pltpu.VMEM((quads * span, tiles * LANES), BF16)],
        ),
        out_shape=jax.ShapeDtypeStruct(out, BF16),
        compiler_params=params(48),
        cost_estimate=cost(steps * step_rows * quads * span * tiles * LANES * 2, 8 << 20),
        name="cross_transform",
    )(mine, *blocks, basis, far)


def physics_kernel(groups, mine_ref, *refs):
    columns, (w_in_ref, w_out_ref) = refs[:groups], refs[groups : groups + 2]
    outs, (spread, found) = refs[groups + 2 : 2 * groups + 2], refs[2 * groups + 2 :]
    per_group, _, rows, _ = columns[0].shape
    chans = groups * per_group
    span = per_group * rows

    def part(offset):
        return pl.ds(pl.multiple_of((mine_ref[0] ^ offset) * span, ROWS), span)

    for offset in range(groups):
        spread[part(offset), :] = columns[offset][:, 0].astype(F32).reshape(span, LANES)
    for group in range(rows // ROWS):
        at = [pl.ds(group * ROWS + row, chans, stride=rows) for row in range(ROWS)]
        block = jnp.concatenate([spread[where, :].astype(BF16) for where in at], axis=1)
        half = mm(w_in_ref[...], block)
        hidden = (half + half * jnp.tanh(half)).astype(BF16)
        tendency = mm(w_out_ref[...], hidden)
        for row in range(ROWS):
            found[at[row], :] = tendency[:, row * LANES : (row + 1) * LANES]
    for offset in range(groups):
        outs[offset][:, 0] = found[part(offset), :].astype(BF16).reshape(per_group, rows, LANES)


def physics(columns, mine, w_in, w_out):
    groups = len(columns)
    per_group, tiles, rows, _ = columns[0].shape
    chans, hidden = w_in.shape
    spec = pl.BlockSpec((per_group, 1, rows, LANES), lambda i, mine: (0, i, 0, 0))
    count = tiles * rows * LANES
    return pl.pallas_call(
        functools.partial(physics_kernel, groups),
        grid_spec=pltpu.PrefetchScalarGridSpec(
            num_scalar_prefetch=1,
            grid=(tiles,),
            in_specs=[spec] * groups
            + [
                pl.BlockSpec((hidden, chans), lambda i, mine: (0, 0)),
                pl.BlockSpec((chans, hidden), lambda i, mine: (0, 0)),
            ],
            out_specs=[spec] * groups,
            scratch_shapes=[pltpu.VMEM((chans * rows, LANES), F32), pltpu.VMEM((chans * rows, LANES), F32)],
        ),
        out_shape=[jax.ShapeDtypeStruct(columns[0].shape, BF16)] * groups,
        compiler_params=params(48),
        cost_estimate=cost(4 * count * chans * hidden, count * chans * 4, count * hidden),
        name="physics",
    )(mine, *columns, w_in.T * jnp.asarray(0.5, BF16), w_out.T)


def gather_kernel(lon_cuts, mine_ref, *refs):
    out_ref = refs[-1]
    tiles = refs[0].shape[1]
    for offset, part in enumerate(refs[:-1]):
        group = mine_ref[0] ^ offset
        for tile in range(tiles):
            out_ref[group % lon_cuts * tiles + tile, group // lon_cuts] = part[:, tile]


def gather_tendency(parts, mine, lat_cuts, lon_cuts):
    shape = parts[0].shape
    chans, tiles, rows, _ = shape
    out = (lon_cuts * tiles, lat_cuts, chans, rows, LANES)
    return pl.pallas_call(
        functools.partial(gather_kernel, lon_cuts),
        grid_spec=pltpu.PrefetchScalarGridSpec(
            num_scalar_prefetch=1,
            grid=(1,),
            in_specs=[pl.BlockSpec(shape, lambda i, mine: (0, 0, 0, 0))] * len(parts),
            out_specs=pl.BlockSpec(out, lambda i, mine: (0, 0, 0, 0, 0)),
        ),
        out_shape=jax.ShapeDtypeStruct(out, BF16),
        compiler_params=params(48),
        cost_estimate=cost(0, 4 * len(parts) * parts[0].size),
        name="gather_tendency",
    )(mine, *parts)


def spectral_kernel(geometry, points, pairs_ref, got_ref, more_ref, legendre_ref, diffusion_ref, out_ref,
                    rows_ref, near_ref, far_ref, cross_ref, block_ref, high_ref, low_ref):
    groups, bands, slots, per_group, lats, folds, lon_cuts = geometry
    half = pairs_ref[slots]
    quads = groups // 2
    part = lats // 2
    rows = part * lon_cuts // quads
    devices = groups * bands
    per_device = 4 * slots
    fold_rows = per_device // folds
    width = per_group * lats
    degrees = legendre_ref.shape[1]
    waves = degrees - 1
    padded = high_ref.shape[0]
    slot = pl.program_id(0)
    chans = groups * per_group
    spans = [(tile, tile * LANES, min(LANES, width - tile * LANES)) for tile in range(rows_ref.shape[0])]
    fill = rows_ref.shape[0] * LANES - width

    def unpack(target, source, past, count, wide, pack):
        for device in range(source.shape[0]):
            for fold in range(pack):
                start = device * count * pack + fold * count
                for tile in range(target.shape[0]):
                    lanes = min(LANES, wide - tile * LANES)
                    at = fold * wide + tile * LANES
                    target[tile, start : start + count, 0:lanes] = source[
                        device, past : past + count, at : at + lanes
                    ].astype(F32)

    near_rows = got_ref.shape[1]
    cross_rows = more_ref.shape[1] - near_rows

    @pl.when(slot == 0)
    def _():
        near = per_group * part
        unpack(near_ref, got_ref, 0, near_rows, near, got_ref.shape[2] // near)
        unpack(far_ref, more_ref, cross_rows, near_rows, near, got_ref.shape[2] // near)
        unpack(cross_ref, more_ref, 0, cross_rows, per_group * rows, got_ref.shape[2] // (per_group * rows))
        high_ref[...] = jnp.zeros_like(high_ref)
        low_ref[...] = jnp.zeros_like(low_ref)

    def rows_of(band, wave):
        return pl.ds(band * per_device + 4 * slot + wave, groups, stride=bands * per_device)

    def read(ref, start, stride):
        where = pl.ds(start, quads, stride=stride)
        return jnp.concatenate([ref[tile, where, :] for tile in range(ref.shape[0])], axis=1)

    stride = bands * per_device
    for wave in range(4):
        for band in range(bands):
            at = band * per_device + 4 * slot + wave
            own = read(near_ref, half * (quads * stride) + at, stride)
            other = read(near_ref, (1 - half) * (quads * stride) + at, stride)
            far = read(far_ref, at, stride)
            cross = []
            for cut in range(quads // lon_cuts):
                total = None
                for lon in range(lon_cuts):
                    source = (cut * lon_cuts + lon) * bands + band
                    term = read(cross_ref, source * quads * per_device + 4 * slot + wave, per_device)
                    total = term if total is None else total + term
                cross.append(total)
            for chan in range(per_group):
                lanes = slice(chan * part, (chan + 1) * part)
                crossed = jnp.concatenate([cut[:, chan * rows : (chan + 1) * rows] for cut in cross], axis=1)
                here = jnp.concatenate([own[:, lanes], crossed], axis=0)
                there = jnp.concatenate([far[:, lanes], other[:, lanes]], axis=0)
                row = (wave * per_group + chan) * groups
                first_lat = band * lats
                block_ref[row : row + groups, first_lat : first_lat + part] = jnp.where(half == 0, here, there)
                block_ref[row : row + groups, first_lat + part : first_lat + lats] = jnp.where(half == 0, there, here)
    high, low = halves(legendre_ref[0])
    high_ref[0:degrees, :] = high
    low_ref[0:degrees, :] = low
    fields = block_ref[...].astype(BF16)
    projected = mm(fields, low_ref[...], NT) + mm(fields, high_ref[...], NT)
    pair = pairs_ref[slot]
    row = lax.broadcasted_iota(jnp.int32, (1, padded), 1)
    first = row < waves - pair
    degree = jnp.where(first, pair + row, row - 1).astype(F32)
    scaled = degree * (degree + 1.0) / F32(waves * (waves + 1))
    wavenum = jnp.where(first, pair, waves - 1 - pair)
    weight = jnp.where(wavenum == 0, F32(1.0 / points), F32(2.0 / points))
    damping = jnp.exp(-diffusion_ref[...] * scaled) * weight
    upper, lower = [], []
    for part in range(2):
        one = projected[part * chans : (part + 1) * chans]
        two = projected[(2 + part) * chans : (3 + part) * chans]
        kept = jnp.where(first, one, two) * damping
        upper.append(jnp.where(first, kept, 0.0))
        lower.append(jnp.where(first, 0.0, kept))
    spec_high, spec_low = halves(jnp.concatenate(upper + lower, axis=0))
    back = mm(spec_low, high_ref[...]) + mm(spec_high, low_ref[...]) + mm(spec_high, high_ref[...])
    for wave in range(4):
        for band in range(bands):
            starts = [(wave * per_group + chan) * groups for chan in range(per_group)]
            pieces = [back[start : start + groups, band * lats : (band + 1) * lats] for start in starts]
            if fill:
                pieces.append(jnp.zeros((groups, fill), F32))
            line = jnp.concatenate(pieces, axis=1)
            line = jnp.where(half == 0, line, jnp.concatenate([line[quads:], line[:quads]], axis=0))
            for tile, at, _ in spans:
                rows_ref[tile, rows_of(band, wave), :] = line[:, at : at + LANES]

    @pl.when(slot == slots - 1)
    def _():
        for device in range(devices):
            for fold in range(folds):
                start = device * per_device + fold * fold_rows
                for tile, at, lanes in spans:
                    out_ref[device, :, fold * width + at : fold * width + at + lanes] = rows_ref[
                        tile, start : start + fold_rows, 0:lanes
                    ].astype(BF16)


def spectral_step(got, more, half, legendre, own_pairs, diffusion, groups, bands, folds, lon_cuts, points):
    slots, degrees, lat_total = legendre.shape
    lats = lat_total // bands
    chans = diffusion.shape[0]
    per_group = chans // groups
    padded = -(-degrees // LANES) * LANES
    by_half = diffusion.reshape(2, groups // 2, per_group)
    by_half = jnp.where(half == 0, by_half, by_half[::-1])
    by_row = by_half.reshape(groups, per_group).T.reshape(chans, 1)
    geometry = (groups, bands, slots, per_group, lats, folds, lon_cuts)
    devices = groups * bands
    near_tiles = -(-per_group * lats // 2 // LANES)
    cross_tiles = -(-per_group * lats * lon_cuts // groups // LANES)
    out = (devices, 4 * slots // folds, per_group * lats * folds)
    whole = lambda i, pairs: (0, 0, 0)
    return pl.pallas_call(
        functools.partial(spectral_kernel, geometry, points),
        grid_spec=pltpu.PrefetchScalarGridSpec(
            num_scalar_prefetch=1,
            grid=(slots,),
            in_specs=[
                pl.BlockSpec(got.shape, whole),
                pl.BlockSpec(more.shape, whole),
                pl.BlockSpec((1, degrees, lat_total), lambda i, pairs: (i, 0, 0)),
                pl.BlockSpec((chans, 1), lambda i, pairs: (0, 0)),
            ],
            out_specs=pl.BlockSpec(out, whole),
            scratch_shapes=[
                pltpu.VMEM((-(-per_group * lats // LANES), devices * 4 * slots, LANES), F32),
                pltpu.VMEM((near_tiles, devices * 4 * slots, LANES), F32),
                pltpu.VMEM((near_tiles, devices // 2 * 4 * slots, LANES), F32),
                pltpu.VMEM((cross_tiles, devices // 2 * (groups // 2) * 4 * slots, LANES), F32),
                pltpu.VMEM((4 * chans, lat_total), F32),
                pltpu.VMEM((padded, lat_total), BF16),
                pltpu.VMEM((padded, lat_total), BF16),
            ],
        ),
        out_shape=jax.ShapeDtypeStruct(out, BF16),
        compiler_params=params(48),
        cost_estimate=cost(40 * slots * chans * degrees * lat_total, slots * degrees * lat_total * 4),
        name="spectral_step",
    )(jnp.concatenate([own_pairs, half]), got, more, legendre, by_row)


def inverse_kernel(geometry, back_ref, basis_ref, tendency_ref, out_ref, rows_ref, turned):
    devices, fold_rows, folds, width = geometry
    chans, lats, step_lons = out_ref.shape
    _, lat_cuts, _, rows, _ = tendency_ref.shape

    @pl.when(pl.program_id(0) == 0)
    def _():
        rows_ref[...] = jnp.zeros_like(rows_ref)
        for device in range(devices):
            for fold in range(folds):
                start = (device * folds + fold) * fold_rows
                rows_ref[start : start + fold_rows, 0:width] = back_ref[
                    device, :, fold * width : (fold + 1) * width
                ]
        turned[...] = rows_ref[...].T

    waves = turned[0:width, :]
    found = mm(waves, basis_ref[...])
    found = found.reshape(chans, lats, step_lons)
    for part in range(step_lons // LANES):
        for cut in range(lat_cuts):
            at = slice(cut * rows, (cut + 1) * rows)
            lanes = slice(part * LANES, (part + 1) * LANES)
            out_ref[:, at, lanes] = found[:, at, lanes] + tendency_ref[part, cut].astype(F32)


def inverse_transform(back, basis, tendency, shape, step_lons):
    chans, lats, lons = shape
    devices, fold_rows, wide = back.shape
    width = chans * lats
    folds = wide // width
    total = basis.shape[0]
    padded = -(-width // LANES) * LANES
    geometry = (devices, fold_rows, folds, width)
    return pl.pallas_call(
        functools.partial(inverse_kernel, geometry),
        grid=(lons // step_lons,),
        in_specs=[
            pl.BlockSpec(back.shape, lambda i: (0, 0, 0), pipeline_mode=pl.Buffered(1)),
            pl.BlockSpec((total, step_lons), lambda i: (0, i)),
            pl.BlockSpec((step_lons // LANES,) + tendency.shape[1:], lambda i: (i, 0, 0, 0, 0)),
        ],
        out_specs=pl.BlockSpec((chans, lats, step_lons), lambda i: (0, 0, i)),
        out_shape=jax.ShapeDtypeStruct(shape, F32),
        scratch_shapes=[pltpu.VMEM((total, padded), BF16), pltpu.VMEM((padded, total), BF16)],
        compiler_params=params(48),
        cost_estimate=cost(2 * total * width * lons, total * lons * 2 + width * lons * 6),
        name="inverse_transform",
    )(back, basis, tendency)


def cuts_of(lats, lons, groups):
    for lon_cuts in range(1, groups + 1):
        if groups % lon_cuts or lons % (lon_cuts * LANES):
            continue
        lat_cuts = groups // lon_cuts
        if lats % (lat_cuts * ROWS) == 0:
            return lat_cuts, lon_cuts
    return None


def folds_of(width, per_device):
    folds = LANES // math.gcd(width, LANES)
    return folds if per_device % (folds * 2 * ROWS) == 0 else None


def halves_fit(chans, lats, lons, slots, groups):
    cuts = cuts_of(lats, lons, groups)
    if cuts is None or groups & (groups - 1) or cuts[0] % 2 or lons % (2 * LANES):
        return False
    near, span, per_device = chans * lats // 2, chans * lats // cuts[0], 4 * slots
    folds = LANES // math.gcd(near, LANES)
    rows = groups // 2 * per_device * span
    return (
        folds_of(2 * near, per_device) is not None
        and per_device % (folds * ROWS) == 0
        and span % (2 * ROWS) == 0
        and rows % (folds * near * 2 * ROWS) == 0
        and per_device % (rows // (folds * near)) == 0
    )


def fast(state, pair_of_slot, legendre, diffusion, w_in, w_out):
    groups = lax.axis_size("grp")
    bands = lax.axis_size("band")
    devices = groups * bands
    quads = groups // 2
    chans, lats, lons = state.shape
    slots, degrees, _ = legendre.shape
    waves = degrees - 1
    lat_cuts, lon_cuts = cuts_of(lats, lons, groups)
    folds = folds_of(chans * lats, 4 * slots)
    near_folds = LANES // math.gcd(chans * lats // 2, LANES)
    mine = lax.axis_index("grp")
    device = mine * bands + lax.axis_index("band")
    mine = mine.reshape(1)
    half = mine // quads
    halves_of = [list(range(side * quads * bands, (side + 1) * quads * bands)) for side in range(2)]
    cut = cut_columns(state, mine, lat_cuts, lon_cuts)
    *cut, pairs = lax.optimization_barrier((*cut, pair_of_slot))
    columns = exchange(cut)
    tables = basis_tables(pairs, lons, waves)
    step_rows = min(8, devices // 2) * 4 * slots
    near, far, basis = forward_transform(state, half, tables, devices, near_folds, step_rows)
    got = lax.all_to_all(near, ("grp", "band"), 0, 0, tiled=True)
    crossed = cross_transform(columns[quads:], far, basis, mine, devices, lon_cuts, step_rows)
    more = lax.all_to_all(crossed, ("grp", "band"), 0, 0, tiled=True, axis_index_groups=halves_of)
    tendency = physics(columns, mine, w_in, w_out)
    *tendency, pairs = lax.optimization_barrier((*tendency, pairs))
    tendency = exchange(tendency)
    own_pairs = lax.dynamic_slice_in_dim(pairs, device * slots, slots)
    solved = spectral_step(
        got, more, half, legendre, own_pairs, diffusion, groups, bands, folds, lon_cuts, lons
    )
    back = lax.all_to_all(solved, ("grp", "band"), 0, 0, tiled=True)
    tendency = gather_tendency(tendency, mine, lat_cuts, lon_cuts)
    return inverse_transform(back, basis, tendency, state.shape, 2 * LANES)


def plain_basis(pair_index, points, waves):
    upper_wave = waves - 1 - pair_index
    wavenums = jnp.stack([pair_index, pair_index, upper_wave, upper_wave], axis=1)
    longitude = jnp.arange(points, dtype=jnp.int32)
    phases = wavenums[:, :, None] * longitude[None, None, :] % points
    angles = phases.astype(jnp.float32) * jnp.float32(2.0 * math.pi / points)
    cosine = jnp.cos(angles)
    sine_part = jnp.sin(angles)
    parity = (jnp.arange(4, dtype=jnp.int32) % 2 == 0)[None, :, None]
    forward = jnp.where(parity, cosine, -sine_part) / jnp.float32(points)
    weights = jnp.where(wavenums == 0, jnp.float32(1.0), jnp.float32(2.0))[:, :, None]
    inverse = jnp.where(parity, cosine, -sine_part) * weights
    return (forward, inverse)


def plain_spectral_step(fields, legendre, pair_index, diffusion):
    waves = legendre.shape[1] - 1
    projected = jnp.einsum("kjcl,krl->kjcr", fields, legendre, precision=lax.Precision.HIGHEST)
    row_index = jnp.arange(legendre.shape[1], dtype=jnp.int32)
    first_part = row_index[None, :] < (waves - pair_index)[:, None]
    degree = jnp.where(
        first_part, pair_index[:, None] + row_index[None, :], row_index[None, :] - 1
    ).astype(jnp.float32)
    scaled = degree * (degree + 1.0) / jnp.float32(waves * (waves + 1))
    damping = jnp.exp(-diffusion[None, :, None] * scaled[:, None, :])
    keep_first = first_part[:, None, None, :]
    filtered = jnp.where(keep_first, projected[:, 0:2], projected[:, 2:4]) * damping[:, None]
    nothing = jnp.zeros_like(filtered)
    coeffs = jnp.concatenate(
        [jnp.where(keep_first, filtered, nothing), jnp.where(keep_first, nothing, filtered)], axis=1
    )
    return jnp.einsum("kjcr,krl->kjcl", coeffs, legendre, precision=lax.Precision.HIGHEST)


def plain(state, pair_of_slot, legendre, diffusion, w_in, w_out):
    groups = lax.axis_size("grp")
    bands = lax.axis_size("band")
    part_chans, lat_rows, lon_total = state.shape
    slot_count = legendre.shape[0]
    lat_total = legendre.shape[2]
    column_block = lax.all_to_all(
        state.astype(jnp.bfloat16), "grp", split_axis=2, concat_axis=0, tiled=True
    )
    channels = column_block.shape[0]
    lon_cols = column_block.shape[2]
    columns = column_block.reshape(channels, lat_rows * lon_cols)
    hidden = lax.dot_general(
        w_in, columns, (((0,), (0,)), ((), ())), preferred_element_type=jnp.float32
    )
    hidden = jax.nn.silu(hidden).astype(jnp.bfloat16)
    tendency = lax.dot_general(
        w_out, hidden, (((0,), (0,)), ((), ())), preferred_element_type=jnp.float32
    )
    tendency = tendency.reshape(channels, lat_rows, lon_cols)
    forward, inverse = plain_basis(pair_of_slot, lon_total, legendre.shape[1] - 1)
    total_slots = forward.shape[0]
    flat_rows = state.reshape(part_chans * lat_rows, lon_total)
    spectra = lax.dot_general(
        forward.reshape(total_slots * 4, lon_total),
        flat_rows,
        (((1,), (1,)), ((), ())),
        precision=lax.Precision.HIGHEST,
    )
    spectra = spectra.reshape(groups, bands, slot_count, 4, part_chans, lat_rows)
    gathered = lax.all_to_all(
        lax.all_to_all(spectra, "grp", split_axis=0, concat_axis=4, tiled=True),
        "band",
        split_axis=1,
        concat_axis=5,
        tiled=True,
    )
    device = lax.axis_index("grp") * bands + lax.axis_index("band")
    own_pairs = lax.dynamic_slice_in_dim(pair_of_slot, device * slot_count, slot_count)
    solved = plain_spectral_step(
        gathered.reshape(slot_count, 4, channels, lat_total), legendre, own_pairs, diffusion
    )
    solved = solved.reshape(1, 1, slot_count, 4, channels, lat_total)
    returned = lax.all_to_all(
        lax.all_to_all(solved, "grp", split_axis=4, concat_axis=0, tiled=True),
        "band",
        split_axis=5,
        concat_axis=1,
        tiled=True,
    )
    coef_flat = returned.reshape(total_slots * 4, part_chans * lat_rows)
    dynamics = lax.dot_general(
        coef_flat,
        inverse.reshape(total_slots * 4, lon_total),
        (((0,), (0,)), ((), ())),
        precision=lax.Precision.HIGHEST,
    )
    dynamics = dynamics.reshape(part_chans, lat_rows, lon_total)
    tendency_rows = lax.all_to_all(
        tendency.astype(jnp.bfloat16), "grp", split_axis=0, concat_axis=2, tiled=True
    ).astype(tendency.dtype)
    return dynamics + tendency_rows


def shards(state, pair_of_slot, legendre, diffusion, w_in, w_out):
    chans, lats, lons = state.shape
    fits = halves_fit(chans, lats, lons, legendre.shape[0], lax.axis_size("grp"))
    if not fits:
        return plain(state, pair_of_slot, legendre, diffusion, w_in, w_out)
    return fast(state, pair_of_slot, legendre, diffusion, w_in, w_out)


def solution(mesh):
    return jax.shard_map(
        shards,
        mesh=mesh,
        in_specs=(P("grp", "band", None), P(), P(("grp", "band"), None, None), P(), P(), P()),
        out_specs=P("grp", "band", None),
        check_vma=False,
    )
```

```python
import functools
import math

import jax
import jax.numpy as jnp
from jax import lax
from jax.experimental import pallas as pl
from jax.experimental.pallas import tpu as pltpu
from jax.sharding import PartitionSpec as P


LANES = 128
ROWS = 8
F32 = jnp.float32
BF16 = jnp.bfloat16
NT = (((1,), (1,)), ((), ()))
NN = (((1,), (0,)), ((), ()))


def mm(a, b, dims=NN):
    return lax.dot_general(a, b, dims, preferred_element_type=F32)


def halves(value):
    high = value.astype(BF16)
    return high, (value - high.astype(F32)).astype(BF16)


def cost(flops, moved, special=0):
    return pl.CostEstimate(flops=int(flops), bytes_accessed=int(moved), transcendentals=int(special))


def params(mib):
    return pltpu.CompilerParams(dimension_semantics=("arbitrary",), vmem_limit_bytes=mib << 20)


def cut_kernel(lon_cuts, first, mine_ref, state_ref, *refs):
    groups = len(refs) - 4
    out_refs, (wide, narrow, arrived, left) = refs[:groups], refs[groups:]
    _, tiles, rows, _ = out_refs[0].shape
    lons = tiles * LANES

    def fetch(offset):
        group = mine_ref[0] ^ (first + offset)
        lat = pl.multiple_of(group // lon_cuts * rows, ROWS)
        lon = pl.multiple_of(group % lon_cuts * lons, LANES)
        block = state_ref.at[:, pl.ds(lat, rows), pl.ds(lon, lons)]
        return pltpu.make_async_copy(block, wide.at[offset], arrived.at[offset])

    def store(offset):
        return pltpu.make_async_copy(narrow.at[offset], out_refs[offset], left.at[offset])

    for offset in range(groups):
        fetch(offset).start()
    for offset in range(groups):
        fetch(offset).wait()
        for tile in range(tiles):
            narrow[offset, :, tile] = wide[offset, :, :, tile * LANES : (tile + 1) * LANES].astype(BF16)
        store(offset).start()
    for offset in range(groups):
        store(offset).wait()


def cut_columns(state, mine, lat_cuts, lon_cuts, first, groups):
    chans, lats, lons = state.shape
    rows, tiles = lats // lat_cuts, lons // lon_cuts // LANES
    block = (chans, tiles, rows, LANES)
    return pl.pallas_call(
        functools.partial(cut_kernel, lon_cuts, first),
        grid_spec=pltpu.PrefetchScalarGridSpec(
            num_scalar_prefetch=1,
            grid=(1,),
            in_specs=[pl.BlockSpec(memory_space=pl.ANY)],
            out_specs=[pl.BlockSpec(memory_space=pl.ANY)] * groups,
            scratch_shapes=[
                pltpu.VMEM((groups, chans, rows, tiles * LANES), F32),
                pltpu.VMEM((groups,) + block, BF16),
                pltpu.SemaphoreType.DMA((groups,)),
                pltpu.SemaphoreType.DMA((groups,)),
            ],
        ),
        out_shape=[jax.ShapeDtypeStruct(block, BF16)] * groups,
        compiler_params=params(60),
        cost_estimate=cost(0, groups * math.prod(block) * 6),
        name="cut_columns",
    )(mine, state)


def exchange(blocks):
    groups = len(blocks)
    got = [blocks[0]] + [None] * (groups - 1)
    for offset in range(groups - 1, 0, -1):
        got[offset] = lax.ppermute(blocks[offset], "grp", [(g, g ^ offset) for g in range(groups)])
    return got


def basis_tables(pair_index, points, waves):
    upper = waves - 1 - pair_index
    wavenums = jnp.stack([pair_index, pair_index, upper, upper], axis=1).reshape(-1, 1)
    odd = (jnp.arange(wavenums.shape[0], dtype=jnp.int32) % 2 == 1)[:, None]
    unit = jnp.float32(2.0 * math.pi / points)

    def angles(at):
        return (wavenums * at[None, :] % points).astype(F32) * unit

    fine = angles(jnp.arange(LANES, dtype=jnp.int32))
    coarse = angles(jnp.arange(points // LANES, dtype=jnp.int32) * LANES)
    cosine, sine = jnp.cos(coarse), jnp.sin(coarse)
    by_cos = jnp.where(odd, -sine, cosine)
    by_sin = jnp.where(odd, -cosine, -sine)
    return jnp.cos(fine), jnp.sin(fine), by_cos, by_sin


def forward_kernel(owners, width, folds, state_ref, cos_ref, sin_ref, by_cos_ref, by_sin_ref,
                   out_ref, high_ref, low_ref, state_high, state_low):
    @pl.when(pl.program_id(0) == 0)
    def _():
        state_high[...], state_low[...] = halves(state_ref[...])

    cosine, sine = cos_ref[...], sin_ref[...]
    for tile in range(by_cos_ref.shape[1]):
        at = slice(tile * LANES, (tile + 1) * LANES)
        wave = by_cos_ref[:, tile : tile + 1] * cosine + by_sin_ref[:, tile : tile + 1] * sine
        high_ref[:, at], low_ref[:, at] = halves(wave)
    found = mm(high_ref[...], state_low[...], NT)
    found += mm(low_ref[...], state_high[...], NT)
    found += mm(high_ref[...], state_high[...], NT)
    rows = out_ref.shape[1]
    for owner in range(owners):
        for fold in range(folds):
            start = (owner * folds + fold) * rows
            out_ref[owner, :, fold * width : (fold + 1) * width] = found[start : start + rows].astype(BF16)


def forward_transform(flat, tables, devices, folds, step_rows):
    width, points = flat.shape
    total = tables[0].shape[0]
    per_owner = total // devices
    rows = per_owner // folds
    owners = step_rows // per_owner
    coarse = points // LANES
    return pl.pallas_call(
        functools.partial(forward_kernel, owners, width, folds),
        grid=(total // step_rows,),
        in_specs=[
            pl.BlockSpec((width, points), lambda i: (0, 0)),
            pl.BlockSpec((step_rows, LANES), lambda i: (i, 0)),
            pl.BlockSpec((step_rows, LANES), lambda i: (i, 0)),
            pl.BlockSpec((step_rows, coarse), lambda i: (i, 0)),
            pl.BlockSpec((step_rows, coarse), lambda i: (i, 0)),
        ],
        out_specs=[
            pl.BlockSpec((owners, rows, folds * width), lambda i: (i, 0, 0)),
            pl.BlockSpec((step_rows, points), lambda i: (i, 0)),
        ],
        out_shape=[
            jax.ShapeDtypeStruct((devices, rows, folds * width), BF16),
            jax.ShapeDtypeStruct((total, points), BF16),
        ],
        scratch_shapes=[
            pltpu.VMEM((step_rows, points), BF16),
            pltpu.VMEM((width, points), BF16),
            pltpu.VMEM((width, points), BF16),
        ],
        compiler_params=params(56),
        cost_estimate=cost(6 * total * width * points, width * points * 4 + total * (points * 4 + width * 2)),
        name="forward_transform",
    )(flat, *tables)


def physics_kernel(groups, mine_ref, *refs):
    columns, (w_in_ref, w_out_ref) = refs[:groups], refs[groups : groups + 2]
    outs, (spread, found) = refs[groups + 2 : 2 * groups + 2], refs[2 * groups + 2 :]
    per_group, _, rows, _ = columns[0].shape
    chans = groups * per_group
    span = per_group * rows

    def part(offset):
        return pl.ds(pl.multiple_of((mine_ref[0] ^ offset) * span, ROWS), span)

    for offset in range(groups):
        spread[part(offset), :] = columns[offset][:, 0].astype(F32).reshape(span, LANES)
    for group in range(rows // ROWS):
        at = [pl.ds(group * ROWS + row, chans, stride=rows) for row in range(ROWS)]
        block = jnp.concatenate([spread[where, :].astype(BF16) for where in at], axis=1)
        half = mm(w_in_ref[...], block)
        hidden = (half + half * jnp.tanh(half)).astype(BF16)
        tendency = mm(w_out_ref[...], hidden)
        for row in range(ROWS):
            found[at[row], :] = tendency[:, row * LANES : (row + 1) * LANES]
    for offset in range(groups):
        outs[offset][:, 0] = found[part(offset), :].astype(BF16).reshape(per_group, rows, LANES)


def physics(columns, mine, w_in, w_out):
    groups = len(columns)
    per_group, tiles, rows, _ = columns[0].shape
    chans, hidden = w_in.shape
    spec = pl.BlockSpec((per_group, 1, rows, LANES), lambda i, mine: (0, i, 0, 0))
    count = tiles * rows * LANES
    return pl.pallas_call(
        functools.partial(physics_kernel, groups),
        grid_spec=pltpu.PrefetchScalarGridSpec(
            num_scalar_prefetch=1,
            grid=(tiles,),
            in_specs=[spec] * groups
            + [
                pl.BlockSpec((hidden, chans), lambda i, mine: (0, 0)),
                pl.BlockSpec((chans, hidden), lambda i, mine: (0, 0)),
            ],
            out_specs=[spec] * groups,
            scratch_shapes=[pltpu.VMEM((chans * rows, LANES), F32), pltpu.VMEM((chans * rows, LANES), F32)],
        ),
        out_shape=[jax.ShapeDtypeStruct(columns[0].shape, BF16)] * groups,
        compiler_params=params(48),
        cost_estimate=cost(4 * count * chans * hidden, count * chans * 4, count * hidden),
        name="physics",
    )(mine, *columns, w_in.T * jnp.asarray(0.5, BF16), w_out.T)


def gather_kernel(lon_cuts, mine_ref, *refs):
    out_ref = refs[-1]
    tiles = refs[0].shape[1]
    for offset, part in enumerate(refs[:-1]):
        group = mine_ref[0] ^ offset
        for tile in range(tiles):
            out_ref[group % lon_cuts * tiles + tile, group // lon_cuts] = part[:, tile]


def gather_tendency(parts, mine, lat_cuts, lon_cuts):
    shape = parts[0].shape
    chans, tiles, rows, _ = shape
    out = (lon_cuts * tiles, lat_cuts, chans, rows, LANES)
    return pl.pallas_call(
        functools.partial(gather_kernel, lon_cuts),
        grid_spec=pltpu.PrefetchScalarGridSpec(
            num_scalar_prefetch=1,
            grid=(1,),
            in_specs=[pl.BlockSpec(shape, lambda i, mine: (0, 0, 0, 0))] * len(parts),
            out_specs=pl.BlockSpec(out, lambda i, mine: (0, 0, 0, 0, 0)),
        ),
        out_shape=jax.ShapeDtypeStruct(out, BF16),
        compiler_params=params(48),
        cost_estimate=cost(0, 4 * len(parts) * parts[0].size),
        name="gather_tendency",
    )(mine, *parts)


def spectral_kernel(geometry, points, pairs_ref, got_ref, legendre_ref, diffusion_ref, out_ref,
                    rows_ref, block_ref, high_ref, low_ref):
    groups, bands, slots, per_group, lats, folds = geometry
    devices = groups * bands
    per_device = 4 * slots
    fold_rows = per_device // folds
    width = per_group * lats
    degrees = legendre_ref.shape[1]
    waves = degrees - 1
    padded = high_ref.shape[0]
    slot = pl.program_id(0)
    chans = groups * per_group
    spans = [(tile, tile * LANES, min(LANES, width - tile * LANES)) for tile in range(rows_ref.shape[0])]
    fill = rows_ref.shape[0] * LANES - width

    @pl.when(slot == 0)
    def _():
        for device in range(devices):
            for fold in range(folds):
                start = device * per_device + fold * fold_rows
                for tile, at, lanes in spans:
                    rows_ref[tile, start : start + fold_rows, 0:lanes] = got_ref[
                        device, :, fold * width + at : fold * width + at + lanes
                    ].astype(F32)
        high_ref[...] = jnp.zeros_like(high_ref)
        low_ref[...] = jnp.zeros_like(low_ref)

    def rows_of(band, wave):
        return pl.ds(band * per_device + 4 * slot + wave, groups, stride=bands * per_device)

    for wave in range(4):
        for band in range(bands):
            piece = jnp.concatenate([rows_ref[tile, rows_of(band, wave), :] for tile, _, _ in spans], axis=1)
            for chan in range(per_group):
                row = (wave * per_group + chan) * groups
                block_ref[row : row + groups, band * lats : (band + 1) * lats] = piece[
                    :, chan * lats : (chan + 1) * lats
                ]
    high, low = halves(legendre_ref[0])
    high_ref[0:degrees, :] = high
    low_ref[0:degrees, :] = low
    fields = block_ref[...].astype(BF16)
    projected = mm(fields, low_ref[...], NT) + mm(fields, high_ref[...], NT)
    pair = pairs_ref[slot]
    row = lax.broadcasted_iota(jnp.int32, (1, padded), 1)
    first = row < waves - pair
    degree = jnp.where(first, pair + row, row - 1).astype(F32)
    scaled = degree * (degree + 1.0) / F32(waves * (waves + 1))
    wavenum = jnp.where(first, pair, waves - 1 - pair)
    weight = jnp.where(wavenum == 0, F32(1.0 / points), F32(2.0 / points))
    damping = jnp.exp(-diffusion_ref[...] * scaled) * weight
    upper, lower = [], []
    for part in range(2):
        one = projected[part * chans : (part + 1) * chans]
        two = projected[(2 + part) * chans : (3 + part) * chans]
        kept = jnp.where(first, one, two) * damping
        upper.append(jnp.where(first, kept, 0.0))
        lower.append(jnp.where(first, 0.0, kept))
    spec_high, spec_low = halves(jnp.concatenate(upper + lower, axis=0))
    back = mm(spec_low, high_ref[...]) + mm(spec_high, low_ref[...]) + mm(spec_high, high_ref[...])
    for wave in range(4):
        for band in range(bands):
            starts = [(wave * per_group + chan) * groups for chan in range(per_group)]
            pieces = [back[start : start + groups, band * lats : (band + 1) * lats] for start in starts]
            if fill:
                pieces.append(jnp.zeros((groups, fill), F32))
            line = jnp.concatenate(pieces, axis=1)
            for tile, at, _ in spans:
                rows_ref[tile, rows_of(band, wave), :] = line[:, at : at + LANES]

    @pl.when(slot == slots - 1)
    def _():
        for device in range(devices):
            for fold in range(folds):
                start = device * per_device + fold * fold_rows
                for tile, at, lanes in spans:
                    out_ref[device, :, fold * width + at : fold * width + at + lanes] = rows_ref[
                        tile, start : start + fold_rows, 0:lanes
                    ].astype(BF16)


def spectral_step(got, legendre, own_pairs, diffusion, groups, bands, folds, points):
    slots, degrees, lat_total = legendre.shape
    lats = lat_total // bands
    chans = diffusion.shape[0]
    per_group = chans // groups
    padded = -(-degrees // LANES) * LANES
    by_row = diffusion.reshape(groups, per_group).T.reshape(chans, 1)
    geometry = (groups, bands, slots, per_group, lats, folds)
    whole = lambda i, pairs: (0, 0, 0)
    return pl.pallas_call(
        functools.partial(spectral_kernel, geometry, points),
        grid_spec=pltpu.PrefetchScalarGridSpec(
            num_scalar_prefetch=1,
            grid=(slots,),
            in_specs=[
                pl.BlockSpec(got.shape, whole),
                pl.BlockSpec((1, degrees, lat_total), lambda i, pairs: (i, 0, 0)),
                pl.BlockSpec((chans, 1), lambda i, pairs: (0, 0)),
            ],
            out_specs=pl.BlockSpec(got.shape, whole),
            scratch_shapes=[
                pltpu.VMEM((-(-per_group * lats // LANES), groups * bands * 4 * slots, LANES), F32),
                pltpu.VMEM((4 * chans, lat_total), F32),
                pltpu.VMEM((padded, lat_total), BF16),
                pltpu.VMEM((padded, lat_total), BF16),
            ],
        ),
        out_shape=jax.ShapeDtypeStruct(got.shape, BF16),
        compiler_params=params(48),
        cost_estimate=cost(40 * slots * chans * degrees * lat_total, slots * degrees * lat_total * 4),
        name="spectral_step",
    )(own_pairs, got, legendre, by_row)


def inverse_kernel(geometry, back_ref, basis_ref, tendency_ref, out_ref, rows_ref, turned):
    devices, fold_rows, folds, width = geometry
    chans, lats, step_lons = out_ref.shape
    _, lat_cuts, _, rows, _ = tendency_ref.shape

    @pl.when(pl.program_id(0) == 0)
    def _():
        for device in range(devices):
            for fold in range(folds):
                start = (device * folds + fold) * fold_rows
                rows_ref[start : start + fold_rows, 0:width] = back_ref[
                    device, :, fold * width : (fold + 1) * width
                ]
        turned[...] = rows_ref[...].T

    waves = turned[0:width, :]
    found = mm(waves, basis_ref[...])
    found = found.reshape(chans, lats, step_lons)
    for part in range(step_lons // LANES):
        for cut in range(lat_cuts):
            at = slice(cut * rows, (cut + 1) * rows)
            lanes = slice(part * LANES, (part + 1) * LANES)
            out_ref[:, at, lanes] = found[:, at, lanes] + tendency_ref[part, cut].astype(F32)


def inverse_transform(back, basis, tendency, shape, step_lons):
    chans, lats, lons = shape
    devices, fold_rows, wide = back.shape
    width = chans * lats
    folds = wide // width
    total = basis.shape[0]
    padded = -(-width // LANES) * LANES
    geometry = (devices, fold_rows, folds, width)
    return pl.pallas_call(
        functools.partial(inverse_kernel, geometry),
        grid=(lons // step_lons,),
        in_specs=[
            pl.BlockSpec(back.shape, lambda i: (0, 0, 0), pipeline_mode=pl.Buffered(1)),
            pl.BlockSpec((total, step_lons), lambda i: (0, i)),
            pl.BlockSpec((step_lons // LANES,) + tendency.shape[1:], lambda i: (i, 0, 0, 0, 0)),
        ],
        out_specs=pl.BlockSpec((chans, lats, step_lons), lambda i: (0, 0, i)),
        out_shape=jax.ShapeDtypeStruct(shape, F32),
        scratch_shapes=[pltpu.VMEM((total, padded), BF16), pltpu.VMEM((padded, total), BF16)],
        compiler_params=params(51),
        cost_estimate=cost(2 * total * width * lons, total * lons * 2 + width * lons * 6),
        name="inverse_transform",
    )(back, basis, tendency)


def cuts_of(lats, lons, groups):
    for lon_cuts in range(1, groups + 1):
        if groups % lon_cuts or lons % (lon_cuts * LANES):
            continue
        lat_cuts = groups // lon_cuts
        if lats % (lat_cuts * ROWS) == 0:
            return lat_cuts, lon_cuts
    return None


def folds_of(width, per_device):
    folds = LANES // math.gcd(width, LANES)
    return folds if per_device % (folds * 2 * ROWS) == 0 else None


def fast(state, pair_of_slot, legendre, diffusion, w_in, w_out):
    groups = lax.axis_size("grp")
    bands = lax.axis_size("band")
    devices = groups * bands
    chans, lats, lons = state.shape
    slots, degrees, _ = legendre.shape
    waves = degrees - 1
    lat_cuts, lon_cuts = cuts_of(lats, lons, groups)
    folds = folds_of(chans * lats, 4 * slots)
    mine = lax.axis_index("grp")
    device = mine * bands + lax.axis_index("band")
    mine = mine.reshape(1)
    cut_far = cut_columns(state, mine, lat_cuts, lon_cuts, groups // 2, groups - groups // 2)
    cut = [*cut_columns(state, mine, lat_cuts, lon_cuts, 0, groups // 2), *cut_far]
    cut[0], pairs = lax.optimization_barrier((cut[0], pair_of_slot))
    columns = exchange(cut)
    tables = basis_tables(pairs, lons, waves)
    step_rows = min(8, devices) * 4 * slots
    spectra, basis = forward_transform(state.reshape(chans * lats, lons), tables, devices, folds, step_rows)
    got = lax.all_to_all(spectra, ("grp", "band"), 0, 0, tiled=True)
    tendency = physics(columns, mine, w_in, w_out)
    *tendency, pairs = lax.optimization_barrier((*tendency, pairs))
    tendency = exchange(tendency)
    own_pairs = lax.dynamic_slice_in_dim(pairs, device * slots, slots)
    solved = spectral_step(got, legendre, own_pairs, diffusion, groups, bands, folds, lons)
    back = lax.all_to_all(solved, ("grp", "band"), 0, 0, tiled=True)
    tendency = gather_tendency(tendency, mine, lat_cuts, lon_cuts)
    return inverse_transform(back, basis, tendency, state.shape, lons // 2)


def plain_basis(pair_index, points, waves):
    upper_wave = waves - 1 - pair_index
    wavenums = jnp.stack([pair_index, pair_index, upper_wave, upper_wave], axis=1)
    longitude = jnp.arange(points, dtype=jnp.int32)
    phases = wavenums[:, :, None] * longitude[None, None, :] % points
    angles = phases.astype(jnp.float32) * jnp.float32(2.0 * math.pi / points)
    cosine = jnp.cos(angles)
    sine_part = jnp.sin(angles)
    parity = (jnp.arange(4, dtype=jnp.int32) % 2 == 0)[None, :, None]
    forward = jnp.where(parity, cosine, -sine_part) / jnp.float32(points)
    weights = jnp.where(wavenums == 0, jnp.float32(1.0), jnp.float32(2.0))[:, :, None]
    inverse = jnp.where(parity, cosine, -sine_part) * weights
    return (forward, inverse)


def plain_spectral_step(fields, legendre, pair_index, diffusion):
    waves = legendre.shape[1] - 1
    projected = jnp.einsum("kjcl,krl->kjcr", fields, legendre, precision=lax.Precision.HIGHEST)
    row_index = jnp.arange(legendre.shape[1], dtype=jnp.int32)
    first_part = row_index[None, :] < (waves - pair_index)[:, None]
    degree = jnp.where(
        first_part, pair_index[:, None] + row_index[None, :], row_index[None, :] - 1
    ).astype(jnp.float32)
    scaled = degree * (degree + 1.0) / jnp.float32(waves * (waves + 1))
    damping = jnp.exp(-diffusion[None, :, None] * scaled[:, None, :])
    keep_first = first_part[:, None, None, :]
    filtered = jnp.where(keep_first, projected[:, 0:2], projected[:, 2:4]) * damping[:, None]
    nothing = jnp.zeros_like(filtered)
    coeffs = jnp.concatenate(
        [jnp.where(keep_first, filtered, nothing), jnp.where(keep_first, nothing, filtered)], axis=1
    )
    return jnp.einsum("kjcr,krl->kjcl", coeffs, legendre, precision=lax.Precision.HIGHEST)


def plain(state, pair_of_slot, legendre, diffusion, w_in, w_out):
    groups = lax.axis_size("grp")
    bands = lax.axis_size("band")
    part_chans, lat_rows, lon_total = state.shape
    slot_count = legendre.shape[0]
    lat_total = legendre.shape[2]
    column_block = lax.all_to_all(
        state.astype(jnp.bfloat16), "grp", split_axis=2, concat_axis=0, tiled=True
    )
    channels = column_block.shape[0]
    lon_cols = column_block.shape[2]
    columns = column_block.reshape(channels, lat_rows * lon_cols)
    hidden = lax.dot_general(
        w_in, columns, (((0,), (0,)), ((), ())), preferred_element_type=jnp.float32
    )
    hidden = jax.nn.silu(hidden).astype(jnp.bfloat16)
    tendency = lax.dot_general(
        w_out, hidden, (((0,), (0,)), ((), ())), preferred_element_type=jnp.float32
    )
    tendency = tendency.reshape(channels, lat_rows, lon_cols)
    forward, inverse = plain_basis(pair_of_slot, lon_total, legendre.shape[1] - 1)
    total_slots = forward.shape[0]
    flat_rows = state.reshape(part_chans * lat_rows, lon_total)
    spectra = lax.dot_general(
        forward.reshape(total_slots * 4, lon_total),
        flat_rows,
        (((1,), (1,)), ((), ())),
        precision=lax.Precision.HIGHEST,
    )
    spectra = spectra.reshape(groups, bands, slot_count, 4, part_chans, lat_rows)
    gathered = lax.all_to_all(
        lax.all_to_all(spectra, "grp", split_axis=0, concat_axis=4, tiled=True),
        "band",
        split_axis=1,
        concat_axis=5,
        tiled=True,
    )
    device = lax.axis_index("grp") * bands + lax.axis_index("band")
    own_pairs = lax.dynamic_slice_in_dim(pair_of_slot, device * slot_count, slot_count)
    solved = plain_spectral_step(
        gathered.reshape(slot_count, 4, channels, lat_total), legendre, own_pairs, diffusion
    )
    solved = solved.reshape(1, 1, slot_count, 4, channels, lat_total)
    returned = lax.all_to_all(
        lax.all_to_all(solved, "grp", split_axis=4, concat_axis=0, tiled=True),
        "band",
        split_axis=5,
        concat_axis=1,
        tiled=True,
    )
    coef_flat = returned.reshape(total_slots * 4, part_chans * lat_rows)
    dynamics = lax.dot_general(
        coef_flat,
        inverse.reshape(total_slots * 4, lon_total),
        (((0,), (0,)), ((), ())),
        precision=lax.Precision.HIGHEST,
    )
    dynamics = dynamics.reshape(part_chans, lat_rows, lon_total)
    tendency_rows = lax.all_to_all(
        tendency.astype(jnp.bfloat16), "grp", split_axis=0, concat_axis=2, tiled=True
    ).astype(tendency.dtype)
    return dynamics + tendency_rows


def shards(state, pair_of_slot, legendre, diffusion, w_in, w_out):
    chans, lats, lons = state.shape
    groups = lax.axis_size("grp")
    fits = groups & (groups - 1) == 0 and lats % ROWS == 0 and lons % (2 * LANES) == 0
    fits = fits and cuts_of(lats, lons, groups) is not None
    fits = fits and folds_of(chans * lats, 4 * legendre.shape[0]) is not None
    if not fits:
        return plain(state, pair_of_slot, legendre, diffusion, w_in, w_out)
    return fast(state, pair_of_slot, legendre, diffusion, w_in, w_out)


def solution(mesh):
    return jax.shard_map(
        shards,
        mesh=mesh,
        in_specs=(P("grp", "band", None), P(), P(("grp", "band"), None, None), P(), P(), P()),
        out_specs=P("grp", "band", None),
        check_vma=False,
    )
```

```python
import functools
import math

import jax
import jax.numpy as jnp
from jax import lax
from jax.experimental import pallas as pl
from jax.experimental.pallas import tpu as pltpu
from jax.sharding import PartitionSpec as P


LANES = 128
ROWS = 8
F32 = jnp.float32
BF16 = jnp.bfloat16
NT = (((1,), (1,)), ((), ()))
NN = (((1,), (0,)), ((), ()))


def mm(a, b, dims=NN):
    return lax.dot_general(a, b, dims, preferred_element_type=F32)


def halves(value):
    high = value.astype(BF16)
    return high, (value - high.astype(F32)).astype(BF16)


def cost(flops, moved, special=0):
    return pl.CostEstimate(flops=int(flops), bytes_accessed=int(moved), transcendentals=int(special))


def params(mib):
    return pltpu.CompilerParams(dimension_semantics=("arbitrary",), vmem_limit_bytes=mib << 20)


def cut_kernel(lon_cuts, first, mine_ref, state_ref, *refs):
    groups = len(refs) - 4
    out_refs, (wide, narrow, arrived, left) = refs[:groups], refs[groups:]
    _, tiles, rows, _ = out_refs[0].shape
    lons = tiles * LANES

    def fetch(offset):
        group = mine_ref[0] ^ (first + offset)
        lat = pl.multiple_of(group // lon_cuts * rows, ROWS)
        lon = pl.multiple_of(group % lon_cuts * lons, LANES)
        block = state_ref.at[:, pl.ds(lat, rows), pl.ds(lon, lons)]
        return pltpu.make_async_copy(block, wide.at[offset], arrived.at[offset])

    def store(offset):
        return pltpu.make_async_copy(narrow.at[offset], out_refs[offset], left.at[offset])

    for offset in range(groups):
        fetch(offset).start()
    for offset in range(groups):
        fetch(offset).wait()
        for tile in range(tiles):
            narrow[offset, :, tile] = wide[offset, :, :, tile * LANES : (tile + 1) * LANES].astype(BF16)
        store(offset).start()
    for offset in range(groups):
        store(offset).wait()


def cut_columns(state, mine, lat_cuts, lon_cuts, first, groups):
    chans, lats, lons = state.shape
    rows, tiles = lats // lat_cuts, lons // lon_cuts // LANES
    block = (chans, tiles, rows, LANES)
    return pl.pallas_call(
        functools.partial(cut_kernel, lon_cuts, first),
        grid_spec=pltpu.PrefetchScalarGridSpec(
            num_scalar_prefetch=1,
            grid=(1,),
            in_specs=[pl.BlockSpec(memory_space=pl.ANY)],
            out_specs=[pl.BlockSpec(memory_space=pl.ANY)] * groups,
            scratch_shapes=[
                pltpu.VMEM((groups, chans, rows, tiles * LANES), F32),
                pltpu.VMEM((groups,) + block, BF16),
                pltpu.SemaphoreType.DMA((groups,)),
                pltpu.SemaphoreType.DMA((groups,)),
            ],
        ),
        out_shape=[jax.ShapeDtypeStruct(block, BF16)] * groups,
        compiler_params=params(60),
        cost_estimate=cost(0, groups * math.prod(block) * 6),
        name="cut_columns",
    )(mine, state)


def exchange(blocks):
    groups = len(blocks)
    got = [blocks[0]] + [None] * (groups - 1)
    for offset in range(groups - 1, 0, -1):
        got[offset] = lax.ppermute(blocks[offset], "grp", [(g, g ^ offset) for g in range(groups)])
    return got


def basis_tables(pair_index, points, waves):
    upper = waves - 1 - pair_index
    odd_pair = pair_index % 2 == 1
    ordered = [jnp.where(odd_pair, upper, pair_index), jnp.where(odd_pair, pair_index, upper)]
    wavenums = jnp.repeat(jnp.concatenate(ordered), 2)[:, None]
    second = (jnp.arange(wavenums.shape[0], dtype=jnp.int32) % 2 == 1)[:, None]
    unit = jnp.float32(2.0 * math.pi / points)

    def angles(at):
        return (wavenums * at[None, :] % points).astype(F32) * unit

    fine = angles(jnp.arange(LANES, dtype=jnp.int32))
    coarse = angles(jnp.arange(points // 2 // LANES, dtype=jnp.int32) * LANES)
    cosine, sine = jnp.cos(coarse), jnp.sin(coarse)
    by_cos = jnp.where(second, -sine, cosine)
    by_sin = jnp.where(second, -cosine, -sine)
    tables = (jnp.cos(fine), jnp.sin(fine), by_cos, by_sin)
    return [table.reshape(2, -1, table.shape[1]) for table in tables]


def forward_kernel(owners, width, state_ref, cos_ref, sin_ref, by_cos_ref, by_sin_ref,
                   out_ref, high_ref, low_ref, state_high, state_low):
    points = high_ref.shape[2]

    @pl.when(pl.program_id(0) == 0)
    def _():
        left, right = state_ref[:, 0:points], state_ref[:, points : 2 * points]
        state_high[0], state_low[0] = halves(left + right)
        state_high[1], state_low[1] = halves(left - right)

    rows = out_ref.shape[1]
    for parity in range(2):
        cosine, sine = cos_ref[parity], sin_ref[parity]
        for tile in range(by_cos_ref.shape[2]):
            at = slice(tile * LANES, (tile + 1) * LANES)
            by_cos, by_sin = by_cos_ref[parity, :, tile : tile + 1], by_sin_ref[parity, :, tile : tile + 1]
            high_ref[parity, :, at], low_ref[:, at] = halves(by_cos * cosine + by_sin * sine)
        found = mm(high_ref[parity], state_low[parity], NT)
        found += mm(low_ref[...], state_high[parity], NT)
        found += mm(high_ref[parity], state_high[parity], NT)
        for owner in range(owners):
            out_ref[owner, :, parity * width : (parity + 1) * width] = found[
                owner * rows : (owner + 1) * rows
            ].astype(BF16)


def forward_transform(flat, tables, devices, owners):
    width, points = flat.shape
    total = tables[0].shape[1]
    rows = total // devices
    step_rows = owners * rows
    coarse = points // 2 // LANES
    return pl.pallas_call(
        functools.partial(forward_kernel, owners, width),
        grid=(devices // owners,),
        in_specs=[
            pl.BlockSpec((width, points), lambda i: (0, 0)),
            pl.BlockSpec((2, step_rows, LANES), lambda i: (0, i, 0)),
            pl.BlockSpec((2, step_rows, LANES), lambda i: (0, i, 0)),
            pl.BlockSpec((2, step_rows, coarse), lambda i: (0, i, 0)),
            pl.BlockSpec((2, step_rows, coarse), lambda i: (0, i, 0)),
        ],
        out_specs=[
            pl.BlockSpec((owners, rows, 2 * width), lambda i: (i, 0, 0)),
            pl.BlockSpec((2, step_rows, points // 2), lambda i: (0, i, 0)),
        ],
        out_shape=[
            jax.ShapeDtypeStruct((devices, rows, 2 * width), BF16),
            jax.ShapeDtypeStruct((2, total, points // 2), BF16),
        ],
        scratch_shapes=[
            pltpu.VMEM((step_rows, points // 2), BF16),
            pltpu.VMEM((2, width, points // 2), BF16),
            pltpu.VMEM((2, width, points // 2), BF16),
        ],
        compiler_params=params(56),
        cost_estimate=cost(6 * total * width * points, width * points * 4 + total * (points * 2 + width * 4)),
        name="forward_transform",
    )(flat, *tables)


def physics_kernel(groups, mine_ref, *refs):
    columns, (w_in_ref, w_out_ref) = refs[:groups], refs[groups : groups + 2]
    outs, (spread, found) = refs[groups + 2 : 2 * groups + 2], refs[2 * groups + 2 :]
    per_group, _, rows, _ = columns[0].shape
    chans = groups * per_group
    span = per_group * rows

    def part(offset):
        return pl.ds(pl.multiple_of((mine_ref[0] ^ offset) * span, ROWS), span)

    for offset in range(groups):
        spread[part(offset), :] = columns[offset][:, 0].astype(F32).reshape(span, LANES)
    for group in range(rows // ROWS):
        at = [pl.ds(group * ROWS + row, chans, stride=rows) for row in range(ROWS)]
        block = jnp.concatenate([spread[where, :].astype(BF16) for where in at], axis=1)
        half = mm(w_in_ref[...], block)
        hidden = (half + half * jnp.tanh(half)).astype(BF16)
        tendency = mm(w_out_ref[...], hidden)
        for row in range(ROWS):
            found[at[row], :] = tendency[:, row * LANES : (row + 1) * LANES]
    for offset in range(groups):
        outs[offset][:, 0] = found[part(offset), :].astype(BF16).reshape(per_group, rows, LANES)


def physics(columns, mine, w_in, w_out):
    groups = len(columns)
    per_group, tiles, rows, _ = columns[0].shape
    chans, hidden = w_in.shape
    spec = pl.BlockSpec((per_group, 1, rows, LANES), lambda i, mine: (0, i, 0, 0))
    count = tiles * rows * LANES
    return pl.pallas_call(
        functools.partial(physics_kernel, groups),
        grid_spec=pltpu.PrefetchScalarGridSpec(
            num_scalar_prefetch=1,
            grid=(tiles,),
            in_specs=[spec] * groups
            + [
                pl.BlockSpec((hidden, chans), lambda i, mine: (0, 0)),
                pl.BlockSpec((chans, hidden), lambda i, mine: (0, 0)),
            ],
            out_specs=[spec] * groups,
            scratch_shapes=[pltpu.VMEM((chans * rows, LANES), F32), pltpu.VMEM((chans * rows, LANES), F32)],
        ),
        out_shape=[jax.ShapeDtypeStruct(columns[0].shape, BF16)] * groups,
        compiler_params=params(60),
        cost_estimate=cost(4 * count * chans * hidden, count * chans * 4, count * hidden),
        name="physics",
    )(mine, *columns, w_in.T * jnp.asarray(0.5, BF16), w_out.T)


def gather_kernel(lon_cuts, mine_ref, *refs):
    out_ref = refs[-1]
    tiles = refs[0].shape[1]
    for offset, part in enumerate(refs[:-1]):
        group = mine_ref[0] ^ offset
        for tile in range(tiles):
            out_ref[group % lon_cuts * tiles + tile, group // lon_cuts] = part[:, tile]


def gather_tendency(parts, mine, lat_cuts, lon_cuts):
    shape = parts[0].shape
    chans, tiles, rows, _ = shape
    out = (lon_cuts * tiles, lat_cuts, chans, rows, LANES)
    return pl.pallas_call(
        functools.partial(gather_kernel, lon_cuts),
        grid_spec=pltpu.PrefetchScalarGridSpec(
            num_scalar_prefetch=1,
            grid=(1,),
            in_specs=[pl.BlockSpec(shape, lambda i, mine: (0, 0, 0, 0))] * len(parts),
            out_specs=pl.BlockSpec(out, lambda i, mine: (0, 0, 0, 0, 0)),
        ),
        out_shape=jax.ShapeDtypeStruct(out, BF16),
        compiler_params=params(48),
        cost_estimate=cost(0, 4 * len(parts) * parts[0].size),
        name="gather_tendency",
    )(mine, *parts)


def spectral_kernel(geometry, points, pairs_ref, got_ref, legendre_ref, diffusion_ref, out_ref,
                    rows_ref, block_ref, high_ref, low_ref):
    groups, bands, slots, per_group, lats, folds = geometry
    devices = groups * bands
    per_device = 4 * slots
    fold_rows = per_device // folds
    width = per_group * lats
    degrees = legendre_ref.shape[1]
    waves = degrees - 1
    padded = high_ref.shape[0]
    slot = pl.program_id(0)
    chans = groups * per_group
    spans = [(tile, tile * LANES, min(LANES, width - tile * LANES)) for tile in range(rows_ref.shape[0])]
    fill = rows_ref.shape[0] * LANES - width

    @pl.when(slot == 0)
    def _():
        for device in range(devices):
            for fold in range(folds):
                start = device * per_device + fold * fold_rows
                for tile, at, lanes in spans:
                    rows_ref[tile, start : start + fold_rows, 0:lanes] = got_ref[
                        device, :, fold * width + at : fold * width + at + lanes
                    ].astype(F32)
        high_ref[...] = jnp.zeros_like(high_ref)
        low_ref[...] = jnp.zeros_like(low_ref)

    def rows_of(band, wave):
        row = band * per_device + wave // 2 * fold_rows + 2 * slot + wave % 2
        return pl.ds(row, groups, stride=bands * per_device)

    for wave in range(4):
        for band in range(bands):
            piece = jnp.concatenate([rows_ref[tile, rows_of(band, wave), :] for tile, _, _ in spans], axis=1)
            for chan in range(per_group):
                row = (wave * per_group + chan) * groups
                block_ref[row : row + groups, band * lats : (band + 1) * lats] = piece[
                    :, chan * lats : (chan + 1) * lats
                ]
    high, low = halves(legendre_ref[0])
    high_ref[0:degrees, :] = high
    low_ref[0:degrees, :] = low
    fields = block_ref[...].astype(BF16)
    projected = mm(fields, low_ref[...], NT) + mm(fields, high_ref[...], NT)
    pair = pairs_ref[slot]
    row = lax.broadcasted_iota(jnp.int32, (1, padded), 1)
    first = row < waves - pair
    degree = jnp.where(first, pair + row, row - 1).astype(F32)
    scaled = degree * (degree + 1.0) / F32(waves * (waves + 1))
    wavenum = jnp.where(first, pair, waves - 1 - pair)
    weight = jnp.where(wavenum == 0, F32(1.0 / points), F32(2.0 / points))
    damping = jnp.exp(-diffusion_ref[...] * scaled) * weight
    even = (jnp.where(first, 1, 0) + pair) % 2 == 1
    upper, lower = [], []
    for part in range(2):
        one = projected[part * chans : (part + 1) * chans]
        two = projected[(2 + part) * chans : (3 + part) * chans]
        kept = jnp.where(even, one, two) * damping
        upper.append(jnp.where(even, kept, 0.0))
        lower.append(jnp.where(even, 0.0, kept))
    spec_high, spec_low = halves(jnp.concatenate(upper + lower, axis=0))
    back = mm(spec_low, high_ref[...]) + mm(spec_high, low_ref[...]) + mm(spec_high, high_ref[...])
    for wave in range(4):
        for band in range(bands):
            starts = [(wave * per_group + chan) * groups for chan in range(per_group)]
            pieces = [back[start : start + groups, band * lats : (band + 1) * lats] for start in starts]
            if fill:
                pieces.append(jnp.zeros((groups, fill), F32))
            line = jnp.concatenate(pieces, axis=1)
            for tile, at, _ in spans:
                rows_ref[tile, rows_of(band, wave), :] = line[:, at : at + LANES]

    @pl.when(slot == slots - 1)
    def _():
        for device in range(devices):
            for fold in range(folds):
                start = device * per_device + fold * fold_rows
                for tile, at, lanes in spans:
                    out_ref[device, :, fold * width + at : fold * width + at + lanes] = rows_ref[
                        tile, start : start + fold_rows, 0:lanes
                    ].astype(BF16)


def spectral_step(got, legendre, own_pairs, diffusion, groups, bands, folds, points):
    slots, degrees, lat_total = legendre.shape
    lats = lat_total // bands
    chans = diffusion.shape[0]
    per_group = chans // groups
    padded = -(-degrees // LANES) * LANES
    by_row = diffusion.reshape(groups, per_group).T.reshape(chans, 1)
    geometry = (groups, bands, slots, per_group, lats, folds)
    whole = lambda i, pairs: (0, 0, 0)
    return pl.pallas_call(
        functools.partial(spectral_kernel, geometry, points),
        grid_spec=pltpu.PrefetchScalarGridSpec(
            num_scalar_prefetch=1,
            grid=(slots,),
            in_specs=[
                pl.BlockSpec(got.shape, whole),
                pl.BlockSpec((1, degrees, lat_total), lambda i, pairs: (i, 0, 0)),
                pl.BlockSpec((chans, 1), lambda i, pairs: (0, 0)),
            ],
            out_specs=pl.BlockSpec(got.shape, whole),
            scratch_shapes=[
                pltpu.VMEM((-(-per_group * lats // LANES), groups * bands * 4 * slots, LANES), F32),
                pltpu.VMEM((4 * chans, lat_total), F32),
                pltpu.VMEM((padded, lat_total), BF16),
                pltpu.VMEM((padded, lat_total), BF16),
            ],
        ),
        out_shape=jax.ShapeDtypeStruct(got.shape, BF16),
        compiler_params=params(60),
        cost_estimate=cost(40 * slots * chans * degrees * lat_total, slots * degrees * lat_total * 4),
        name="spectral_step",
    )(own_pairs, got, legendre, by_row)


def inverse_kernel(width, back_ref, basis_ref, tendency_ref, out_ref, rows_ref, turned, differ):
    devices, fold_rows, _ = back_ref.shape
    chans, lats, step_lons = out_ref.shape
    _, lat_cuts, _, rows, _ = tendency_ref.shape
    count = devices * fold_rows

    def put(found):
        found = found.reshape(chans, lats, step_lons)
        for part in range(step_lons // LANES):
            for cut in range(lat_cuts):
                at = slice(cut * rows, (cut + 1) * rows)
                lanes = slice(part * LANES, (part + 1) * LANES)
                out_ref[:, at, lanes] = found[:, at, lanes] + tendency_ref[part, cut].astype(F32)

    @pl.when(pl.program_id(0) == 0)
    def _():
        for parity in range(2):
            for device in range(devices):
                start = parity * count + device * fold_rows
                rows_ref[start : start + fold_rows, 0:width] = back_ref[
                    device, :, parity * width : (parity + 1) * width
                ]
        turned[...] = rows_ref[...].T
        even = mm(turned[0:width, 0:count], basis_ref[0])
        odd = mm(turned[0:width, count : 2 * count], basis_ref[1])
        differ[...] = even - odd
        put(even + odd)

    @pl.when(pl.program_id(0) == 1)
    def _():
        put(differ[...])


def inverse_transform(back, basis, tendency, shape):
    chans, lats, lons = shape
    width = chans * lats
    total = 2 * basis.shape[1]
    padded = -(-width // LANES) * LANES
    return pl.pallas_call(
        functools.partial(inverse_kernel, width),
        grid=(2,),
        in_specs=[
            pl.BlockSpec(back.shape, lambda i: (0, 0, 0), pipeline_mode=pl.Buffered(1)),
            pl.BlockSpec(basis.shape, lambda i: (0, 0, 0), pipeline_mode=pl.Buffered(1)),
            pl.BlockSpec((lons // 2 // LANES,) + tendency.shape[1:], lambda i: (i, 0, 0, 0, 0)),
        ],
        out_specs=pl.BlockSpec((chans, lats, lons // 2), lambda i: (0, 0, i)),
        out_shape=jax.ShapeDtypeStruct(shape, F32),
        scratch_shapes=[
            pltpu.VMEM((total, padded), BF16),
            pltpu.VMEM((padded, total), BF16),
            pltpu.VMEM((width, lons // 2), F32),
        ],
        compiler_params=params(51),
        cost_estimate=cost(total * width * lons, total * lons + width * lons * 6),
        name="inverse_transform",
    )(back, basis, tendency)


def cuts_of(lats, lons, groups):
    for lon_cuts in range(1, groups + 1):
        if groups % lon_cuts or lons % (lon_cuts * LANES):
            continue
        lat_cuts = groups // lon_cuts
        if lats % (lat_cuts * ROWS) == 0:
            return lat_cuts, lon_cuts
    return None


def folds_of(width, per_device):
    folds = LANES // math.gcd(width, LANES)
    return folds if per_device % (folds * 2 * ROWS) == 0 else None


def fast(state, pair_of_slot, legendre, diffusion, w_in, w_out):
    groups = lax.axis_size("grp")
    bands = lax.axis_size("band")
    devices = groups * bands
    chans, lats, lons = state.shape
    slots, degrees, _ = legendre.shape
    waves = degrees - 1
    lat_cuts, lon_cuts = cuts_of(lats, lons, groups)
    folds = folds_of(chans * lats, 4 * slots)
    mine = lax.axis_index("grp")
    device = mine * bands + lax.axis_index("band")
    mine = mine.reshape(1)
    cut_far = cut_columns(state, mine, lat_cuts, lon_cuts, groups // 2, groups - groups // 2)
    cut = [*cut_columns(state, mine, lat_cuts, lon_cuts, 0, groups // 2), *cut_far]
    cut[0], pairs = lax.optimization_barrier((cut[0], pair_of_slot))
    columns = exchange(cut)
    tables = basis_tables(pairs, lons, waves)
    spectra, basis = forward_transform(state.reshape(chans * lats, lons), tables, devices, min(16, devices))
    got = lax.all_to_all(spectra, ("grp", "band"), 0, 0, tiled=True)
    tendency = physics(columns, mine, w_in, w_out)
    *tendency, pairs = lax.optimization_barrier((*tendency, pairs))
    tendency = exchange(tendency)
    own_pairs = lax.dynamic_slice_in_dim(pairs, device * slots, slots)
    solved = spectral_step(got, legendre, own_pairs, diffusion, groups, bands, folds, lons)
    back = lax.all_to_all(solved, ("grp", "band"), 0, 0, tiled=True)
    tendency = gather_tendency(tendency, mine, lat_cuts, lon_cuts)
    return inverse_transform(back, basis, tendency, state.shape)


def plain_basis(pair_index, points, waves):
    upper_wave = waves - 1 - pair_index
    wavenums = jnp.stack([pair_index, pair_index, upper_wave, upper_wave], axis=1)
    longitude = jnp.arange(points, dtype=jnp.int32)
    phases = wavenums[:, :, None] * longitude[None, None, :] % points
    angles = phases.astype(jnp.float32) * jnp.float32(2.0 * math.pi / points)
    cosine = jnp.cos(angles)
    sine_part = jnp.sin(angles)
    parity = (jnp.arange(4, dtype=jnp.int32) % 2 == 0)[None, :, None]
    forward = jnp.where(parity, cosine, -sine_part) / jnp.float32(points)
    weights = jnp.where(wavenums == 0, jnp.float32(1.0), jnp.float32(2.0))[:, :, None]
    inverse = jnp.where(parity, cosine, -sine_part) * weights
    return (forward, inverse)


def plain_spectral_step(fields, legendre, pair_index, diffusion):
    waves = legendre.shape[1] - 1
    projected = jnp.einsum("kjcl,krl->kjcr", fields, legendre, precision=lax.Precision.HIGHEST)
    row_index = jnp.arange(legendre.shape[1], dtype=jnp.int32)
    first_part = row_index[None, :] < (waves - pair_index)[:, None]
    degree = jnp.where(
        first_part, pair_index[:, None] + row_index[None, :], row_index[None, :] - 1
    ).astype(jnp.float32)
    scaled = degree * (degree + 1.0) / jnp.float32(waves * (waves + 1))
    damping = jnp.exp(-diffusion[None, :, None] * scaled[:, None, :])
    keep_first = first_part[:, None, None, :]
    filtered = jnp.where(keep_first, projected[:, 0:2], projected[:, 2:4]) * damping[:, None]
    nothing = jnp.zeros_like(filtered)
    coeffs = jnp.concatenate(
        [jnp.where(keep_first, filtered, nothing), jnp.where(keep_first, nothing, filtered)], axis=1
    )
    return jnp.einsum("kjcr,krl->kjcl", coeffs, legendre, precision=lax.Precision.HIGHEST)


def plain(state, pair_of_slot, legendre, diffusion, w_in, w_out):
    groups = lax.axis_size("grp")
    bands = lax.axis_size("band")
    part_chans, lat_rows, lon_total = state.shape
    slot_count = legendre.shape[0]
    lat_total = legendre.shape[2]
    column_block = lax.all_to_all(
        state.astype(jnp.bfloat16), "grp", split_axis=2, concat_axis=0, tiled=True
    )
    channels = column_block.shape[0]
    lon_cols = column_block.shape[2]
    columns = column_block.reshape(channels, lat_rows * lon_cols)
    hidden = lax.dot_general(
        w_in, columns, (((0,), (0,)), ((), ())), preferred_element_type=jnp.float32
    )
    hidden = jax.nn.silu(hidden).astype(jnp.bfloat16)
    tendency = lax.dot_general(
        w_out, hidden, (((0,), (0,)), ((), ())), preferred_element_type=jnp.float32
    )
    tendency = tendency.reshape(channels, lat_rows, lon_cols)
    forward, inverse = plain_basis(pair_of_slot, lon_total, legendre.shape[1] - 1)
    total_slots = forward.shape[0]
    flat_rows = state.reshape(part_chans * lat_rows, lon_total)
    spectra = lax.dot_general(
        forward.reshape(total_slots * 4, lon_total),
        flat_rows,
        (((1,), (1,)), ((), ())),
        precision=lax.Precision.HIGHEST,
    )
    spectra = spectra.reshape(groups, bands, slot_count, 4, part_chans, lat_rows)
    gathered = lax.all_to_all(
        lax.all_to_all(spectra, "grp", split_axis=0, concat_axis=4, tiled=True),
        "band",
        split_axis=1,
        concat_axis=5,
        tiled=True,
    )
    device = lax.axis_index("grp") * bands + lax.axis_index("band")
    own_pairs = lax.dynamic_slice_in_dim(pair_of_slot, device * slot_count, slot_count)
    solved = plain_spectral_step(
        gathered.reshape(slot_count, 4, channels, lat_total), legendre, own_pairs, diffusion
    )
    solved = solved.reshape(1, 1, slot_count, 4, channels, lat_total)
    returned = lax.all_to_all(
        lax.all_to_all(solved, "grp", split_axis=4, concat_axis=0, tiled=True),
        "band",
        split_axis=5,
        concat_axis=1,
        tiled=True,
    )
    coef_flat = returned.reshape(total_slots * 4, part_chans * lat_rows)
    dynamics = lax.dot_general(
        coef_flat,
        inverse.reshape(total_slots * 4, lon_total),
        (((0,), (0,)), ((), ())),
        precision=lax.Precision.HIGHEST,
    )
    dynamics = dynamics.reshape(part_chans, lat_rows, lon_total)
    tendency_rows = lax.all_to_all(
        tendency.astype(jnp.bfloat16), "grp", split_axis=0, concat_axis=2, tiled=True
    ).astype(tendency.dtype)
    return dynamics + tendency_rows


def shards(state, pair_of_slot, legendre, diffusion, w_in, w_out):
    chans, lats, lons = state.shape
    groups = lax.axis_size("grp")
    fits = groups & (groups - 1) == 0 and lats % ROWS == 0 and lons % (2 * LANES) == 0
    fits = fits and cuts_of(lats, lons, groups) is not None
    fits = fits and folds_of(chans * lats, 4 * legendre.shape[0]) == 2 and legendre.shape[1] % 2 == 1
    if not fits:
        return plain(state, pair_of_slot, legendre, diffusion, w_in, w_out)
    return fast(state, pair_of_slot, legendre, diffusion, w_in, w_out)


def solution(mesh):
    return jax.shard_map(
        shards,
        mesh=mesh,
        in_specs=(P("grp", "band", None), P(), P(("grp", "band"), None, None), P(), P(), P()),
        out_specs=P("grp", "band", None),
        check_vma=False,
    )
```
